32 devices in a mesh: curve: 8 (over y, x, core), group: 4 (over z).
Axes of the slice: x: 2, y: 2, z: 4, core: 2. Of those that a mesh axis runs over, the one named last changes fastest.
Arguments:
- points: bfloat16 [65536, 256], P(('curve', 'group')), may hold values from -9 to 9
- qkv_one: bfloat16 [256, 768], replicated, may hold values from -1.25 to 1.25
- proj_one: bfloat16 [256, 256], replicated, may hold values from -0.375 to 0.375
- up_one: bfloat16 [256, 1024], replicated, may hold values from -0.375 to 0.375
- down_one: bfloat16 [1024, 256], replicated, may hold values from -0.1875 to 0.1875
- hilbert_device: int32 [65536], P(('curve', 'group')), may hold values from 0 to 31, as said below
- hilbert_position: int32 [65536], P(('curve', 'group')), may hold values from 0 to 2047, as said below
- neighbors: int32 [65536, 27], P(('curve', 'group')), may hold values from -1 to 4096, as said below
- conv_two: bfloat16 [6912, 256], replicated, may hold values from -0.09375 to 0.09375
- linear_two: bfloat16 [256, 256], replicated, may hold values from -0.375 to 0.375
Outputs:
- features: bfloat16 [65536, 256], P(('curve', 'group'))
The draws below stay inside these ranges and needn't reach their ends.
Inputs may be any that keep to these rules, and one draw needn't show every extreme that they name: `hilbert_device`: together with hilbert_position it is a permutation of the points; every device's span receives 2048 points; the number of points that device s sends to device d depends only on (d - s) modulo the number of devices, is at most 128, and equals 128 for some pairs in every draw. `hilbert_position`: distinct for the points that go to one device. `neighbors`: -1 marks a missing neighbour; otherwise the neighbour is a point of the crop. Offset 27 // 2 is the point itself; offset 0 is the point 2048 rows before and offset 27 - 1 the point 2048 rows after, where those lie in the crop.
All inputs are finite; a program needn't handle non-finite values.
Results may differ from the reference program's by a relative error of at most 0.015.
The reference program's roundings to bfloat16 on the way count: a program that leaves them out, or rounds other values in their place, can miss the bound.
Values may be sent and summed in bfloat16 or wider, within the bound.
No kernel may reach another device: no remote copies, remote signals or barrier semaphores. Data moves between devices by JAX's collectives and lax.ppermute only.
A program may use at most 128 MiB of HBM per device.

```python
import jax
import jax.numpy as jnp
from jax import lax

C = 256
HEADS = 16
HEAD_DIM = 16
MLP = 1024
PATCH = 1024
NBR = 27
ROWS_DEV = 2048
REACH = 2048
CAP = 128
POINTS = 65536


def draw_points(key, part):
    key_base, key_row, key_col = jax.random.split(jax.random.fold_in(key, 11), 3)
    row_scale = jnp.exp(jax.random.uniform(key_row, (POINTS, 1), jnp.float32, jnp.log(0.3), jnp.log(1.5)))
    col_scale = jnp.exp(jax.random.uniform(key_col, (1, C), jnp.float32, jnp.log(0.3), jnp.log(1.5)))
    base = jnp.clip(jax.random.normal(key_base, (POINTS, C), jnp.float32), -4.0, 4.0)
    return (base * row_scale * col_scale).astype(jnp.bfloat16)


def projection_draw(key, salt):
    key_query = jax.random.fold_in(jax.random.fold_in(key, salt), 0)
    key_value = jax.random.fold_in(jax.random.fold_in(key, salt), 2)
    scale = C ** (-0.5)
    query_key = jax.random.normal(key_query, (C, 2 * C), jnp.float32) * (3.0 * scale)
    value_part = jax.random.normal(key_value, (C, C), jnp.float32) * scale
    matrix = jnp.concatenate([query_key, value_part], axis=1)
    return jnp.clip(matrix, -1.25, 1.25).astype(jnp.bfloat16)


def draw_qkv_one(key, part):
    return projection_draw(key, 21)


def hilbert_parts(key):
    devices = 2 * ROWS_DEV // CAP
    half_cap = CAP // 2
    key_counts, key_star, key_sign, key_send, key_recv = jax.random.split(jax.random.fold_in(key, 7), 5)
    offsets = jax.random.randint(key_counts, (devices // 2,), -half_cap, half_cap + 1)
    star = jax.random.randint(key_star, (), 0, devices // 2)
    sign = jax.random.randint(key_sign, (), 0, 2) * 2 - 1
    offsets = jnp.where(jnp.arange(devices // 2) == star, sign * half_cap, offsets)
    counts = jnp.concatenate([half_cap + offsets, half_cap - offsets])
    ends = jnp.cumsum(counts)
    slots = jnp.arange(ROWS_DEV, dtype=jnp.int32)
    distance = jnp.searchsorted(ends, slots, side='right').astype(jnp.int32)
    send_perm = jax.vmap(lambda sub: jax.random.permutation(sub, ROWS_DEV))(jax.random.split(key_send, devices))
    recv_perm = jax.vmap(lambda sub: jax.random.permutation(sub, ROWS_DEV))(jax.random.split(key_recv, devices))
    source = jnp.arange(devices, dtype=jnp.int32)[:, None]
    target_dev = (source + distance[None, :]) % devices
    target_row = recv_perm[target_dev, slots[None, :]].astype(jnp.int32)
    global_rows = (source * ROWS_DEV + send_perm).reshape(-1)
    device_out = jnp.zeros((POINTS,), jnp.int32).at[global_rows].set(target_dev.reshape(-1).astype(jnp.int32))
    position_out = jnp.zeros((POINTS,), jnp.int32).at[global_rows].set(target_row.reshape(-1))
    return (device_out, position_out)


def draw_hilbert_device(key, part):
    return hilbert_parts(key)[0]


def draw_hilbert_position(key, part):
    return hilbert_parts(key)[1]


def draw_neighbors(key, part):
    key_offset, key_keep = jax.random.split(jax.random.fold_in(key, 31), 2)
    offsets = jax.random.randint(key_offset, (POINTS, NBR), -REACH, REACH + 1)
    column = jnp.arange(NBR)[None, :]
    offsets = jnp.where(column == 0, -REACH, offsets)
    offsets = jnp.where(column == NBR - 1, REACH, offsets)
    offsets = jnp.where(column == NBR // 2, 0, offsets)
    keep = jax.random.randint(key_keep, (POINTS, NBR), 0, 3) > 0
    keep = keep | (column == 0) | (column == NBR - 1) | (column == NBR // 2)
    target = jnp.arange(POINTS)[:, None] + offsets
    inside = (target >= 0) & (target < POINTS)
    return jnp.where(keep & inside, offsets + REACH, -1).astype(jnp.int32)


def noise(own_key, extent, scale, reach, kind=jnp.bfloat16):
    array = scale * jax.random.normal(own_key, extent, jnp.float32)
    return jnp.clip(array, min=-reach, max=reach).astype(kind)


def setup_inputs(seed: int = 0) -> dict:
    seeds = jax.random.split(jax.random.key(seed), 11)
    points = draw_points(jax.random.fold_in(seeds[10], 71), 0)
    qkv_one = draw_qkv_one(jax.random.fold_in(seeds[10], 71), 0)
    proj_one = noise(seeds[2], (C, C), C ** -0.5, 0.375)
    up_one = noise(seeds[3], (C, MLP), C ** -0.5, 0.375)
    down_one = noise(seeds[4], (MLP, C), MLP ** -0.5, 0.1875)
    hilbert_device = draw_hilbert_device(jax.random.fold_in(seeds[10], 71), 0)
    hilbert_position = draw_hilbert_position(jax.random.fold_in(seeds[10], 71), 0)
    neighbors = draw_neighbors(jax.random.fold_in(seeds[10], 71), 0)
    conv_two = noise(seeds[8], (NBR * C, C), (2 * NBR * C // 3) ** -0.5, 0.09375)
    linear_two = noise(seeds[9], (C, C), C ** -0.5, 0.375)
    return dict(points=points, qkv_one=qkv_one, proj_one=proj_one, up_one=up_one, down_one=down_one, hilbert_device=hilbert_device, hilbert_position=hilbert_position, neighbors=neighbors, conv_two=conv_two, linear_two=linear_two)


EPS = 1e-05

def layer_norm(values):
    values = values.astype(jnp.float32)
    center = lax.optimization_barrier(jnp.mean(values, axis=-1, keepdims=True))
    spread = lax.optimization_barrier(jnp.mean((values - center) ** 2, axis=-1, keepdims=True))
    return (values - center) * lax.rsqrt(spread + EPS)

def patch_attention(projected):
    queries = projected[:, :C].reshape(-1, HEADS, HEAD_DIM).astype(jnp.float32)
    keys = projected[:, C:2 * C].reshape(-1, HEADS, HEAD_DIM).astype(jnp.float32)
    values = projected[:, 2 * C:].reshape(-1, HEADS, HEAD_DIM).astype(jnp.float32)
    scores = jnp.einsum('qhd,khd->hqk', queries, keys) * HEAD_DIM ** (-0.5)
    weights = jax.nn.softmax(scores, axis=-1).astype(jnp.bfloat16)
    mixed = jnp.einsum('hqk,khd->qhd', weights.astype(jnp.float32), values)
    return mixed.reshape(-1, C).astype(jnp.bfloat16)

def finish(residual, mixed, proj_w, up_w, down_w):
    after = (residual.astype(jnp.float32) + jnp.dot(mixed, proj_w, preferred_element_type=jnp.float32)).astype(jnp.bfloat16)
    normed = layer_norm(after).astype(jnp.bfloat16)
    hidden = jax.nn.gelu(jnp.dot(normed, up_w, preferred_element_type=jnp.float32), approximate=False).astype(jnp.bfloat16)
    return (after.astype(jnp.float32) + jnp.dot(hidden, down_w, preferred_element_type=jnp.float32)).astype(jnp.bfloat16)

def block(inputs, qkv_w, proj_w, up_w, down_w, offset):
    normed = layer_norm(inputs).astype(jnp.bfloat16)
    projected = jnp.dot(normed, qkv_w, preferred_element_type=jnp.float32).astype(jnp.bfloat16)
    rolled = jnp.roll(projected, -offset, axis=0)
    mixed = lax.map(patch_attention, rolled.reshape(-1, PATCH, 3 * C)).reshape(-1, C)
    mixed = jnp.roll(mixed, offset, axis=0)
    return finish(inputs, mixed, proj_w, up_w, down_w)

def reference(points, qkv_one, proj_one, up_one, down_one, hilbert_device, hilbert_position, neighbors, conv_two, linear_two):
    z_out = block(points, qkv_one, proj_one, up_one, down_one, PATCH // 2)
    target = hilbert_device * ROWS_DEV + hilbert_position
    serial = jnp.zeros((POINTS, C), jnp.bfloat16).at[target].set(z_out)

    def conv_rows(block_index):
        start = (block_index * ROWS_DEV).astype(jnp.int32)
        near = lax.dynamic_slice_in_dim(neighbors, start, ROWS_DEV, 0)
        valid = near >= 0
        index_rows = start + jnp.arange(ROWS_DEV, dtype=jnp.int32)[:, None] + near - REACH
        index_rows = jnp.where(valid, index_rows, 0).astype(jnp.int32)
        gathered = jnp.where(valid[..., None], serial[index_rows], jnp.zeros((), jnp.bfloat16))
        return jnp.dot(gathered.reshape(ROWS_DEV, NBR * C), conv_two, preferred_element_type=jnp.float32).astype(jnp.bfloat16)
    conv = lax.map(conv_rows, jnp.arange(POINTS // ROWS_DEV, dtype=jnp.int32)).reshape(POINTS, C)
    linear = jnp.dot(conv, linear_two, preferred_element_type=jnp.float32)
    return (serial.astype(jnp.float32) + layer_norm(linear)).astype(jnp.bfloat16)
```

```python
import functools

import jax
import jax.numpy as jnp
from jax import lax
from jax.experimental import pallas as pl
from jax.experimental.pallas import tpu as pltpu
from jax.sharding import PartitionSpec as P

HEADS = 16
HEAD_DIM = 16
PATCH = 1024


EPS = 1e-05


def with_halo(cells, sides, width, closed):
    for axis, dim in sides:
        count = lax.axis_size(axis)
        ends = count if closed else count - 1
        head = lax.slice_in_dim(cells, 0, width, axis=dim)
        tail = lax.slice_in_dim(cells, cells.shape[dim] - width, cells.shape[dim], axis=dim)
        cells = jnp.concatenate(
            [
                lax.ppermute(tail, axis, [(i, (i + 1) % count) for i in range(ends)]),
                cells,
                lax.ppermute(head, axis, [((i + 1) % count, i) for i in range(ends)]),
            ],
            axis=dim,
        )
    return cells


def layer_norm(values):
    values = values.astype(jnp.float32)
    center = jnp.mean(values, axis=-1, keepdims=True)
    spread = jnp.mean((values - center) ** 2, axis=-1, keepdims=True)
    return (values - center) * lax.rsqrt(spread + EPS)


def block_attention(queries, keys_all, values_all):
    row_count = queries.shape[0]
    half_patch = PATCH // 2
    block_count = row_count // half_patch
    group_heads = HEADS // 2
    span = group_heads * HEAD_DIM

    def one_block(block_index):
        query_rows = lax.dynamic_slice_in_dim(queries, block_index * half_patch, half_patch, 0)
        start = PATCH * ((block_index + 1) // 2)
        key_rows = lax.dynamic_slice_in_dim(keys_all, start, PATCH, 0)
        value_rows = lax.dynamic_slice_in_dim(values_all, start, PATCH, 0)
        pieces = []
        for group in range(2):
            lower = group * span
            query_group = query_rows[:, lower : lower + span].reshape(
                half_patch, group_heads, HEAD_DIM
            )
            key_group = key_rows[:, lower : lower + span].reshape(PATCH, group_heads, HEAD_DIM)
            value_group = value_rows[:, lower : lower + span].reshape(PATCH, group_heads, HEAD_DIM)
            scores = jnp.einsum(
                "qhd,khd->hqk", query_group, key_group, preferred_element_type=jnp.float32
            ) * HEAD_DIM ** (-0.5)
            weights = jax.nn.softmax(scores, axis=-1).astype(jnp.bfloat16)
            result = jnp.einsum(
                "hqk,khd->qhd", weights, value_group, preferred_element_type=jnp.float32
            ).astype(jnp.bfloat16)
            pieces.append(result.reshape(half_patch, span))
        return jnp.concatenate(pieces, axis=1)

    mixed = lax.map(one_block, jnp.arange(block_count, dtype=jnp.int32))
    return mixed.reshape(row_count, -1)


def finish(residual, mixed, proj_w, up_w, down_w):
    after = (
        residual.astype(jnp.float32) + jnp.dot(mixed, proj_w, preferred_element_type=jnp.float32)
    ).astype(jnp.bfloat16)
    normed = layer_norm(after).astype(jnp.bfloat16)
    hidden = jax.nn.gelu(
        jnp.dot(normed, up_w, preferred_element_type=jnp.float32), approximate=False
    ).astype(jnp.bfloat16)
    return (
        after.astype(jnp.float32) + jnp.dot(hidden, down_w, preferred_element_type=jnp.float32)
    ).astype(jnp.bfloat16)


def conv_kernel(block, offs, rows, idx_ref, left_ref, own_ref, right_ref, w_ref, lin_ref, out_ref, tab, buf, lhs):
    step = pl.program_id(0)
    lanes = 128

    @pl.when(step == 0)
    def _():
        for part, ref in enumerate((left_ref, own_ref, right_ref)):
            for half in range(2):
                tab[pl.ds(2 * part * rows + half, rows, stride=2), :] = ref[:, half * lanes:(half + 1) * lanes].astype(jnp.float32)
        tab[pl.ds(6 * rows, 8), :] = jnp.zeros((8, lanes), jnp.float32)

    start = pl.multiple_of(step * block, block)
    width = 2 * lanes
    mid = offs // 2
    for k, ref in ((0, left_ref), (mid, own_ref), (offs - 1, right_ref)):
        lhs[:, k * width:(k + 1) * width] = ref[pl.ds(start, block), :]

    def one(o):
        base = o * block
        for j in range(block):
            buf[2 * j:2 * j + 2, :] = tab[pl.ds(pl.multiple_of(idx_ref[0, 0, base + j], 2), 2), :]
        for half in range(2):
            lhs[:, pl.ds(pl.multiple_of(o * width + half * lanes, lanes), lanes)] = buf[pl.ds(half, block, stride=2), :].astype(jnp.bfloat16)

    def body(o, carry):
        one(o)
        return carry
    lax.fori_loop(1, mid, body, 0)
    lax.fori_loop(mid + 1, offs - 1, body, 0)
    conv = jnp.dot(lhs[...], w_ref[...], preferred_element_type=jnp.float32).astype(jnp.bfloat16)
    linear = jnp.dot(conv, lin_ref[...], preferred_element_type=jnp.float32)
    center = jnp.mean(linear, axis=-1, keepdims=True)
    d = linear - center
    spread = jnp.mean(d * d, axis=-1, keepdims=True)
    normed = d * lax.rsqrt(spread + EPS)
    out_ref[...] = (own_ref[pl.ds(start, block), :].astype(jnp.float32) + normed).astype(jnp.bfloat16)

def position_conv(idx, left, own, right, w, lin, block):
    rows, ch = own.shape
    offs = w.shape[0] // ch
    vm = pl.BlockSpec(memory_space=pltpu.VMEM)
    return pl.pallas_call(
        functools.partial(conv_kernel, block, offs, rows),
        out_shape=jax.ShapeDtypeStruct((rows, ch), jnp.bfloat16),
        grid=(rows // block,),
        in_specs=[pl.BlockSpec((1, 1, offs * block), lambda i: (i, 0, 0), memory_space=pltpu.SMEM), vm, vm, vm, vm, vm],
        out_specs=pl.BlockSpec((block, ch), lambda i: (i, 0)),
        scratch_shapes=[pltpu.VMEM((6 * rows + 8, 128), jnp.float32), pltpu.VMEM((2 * block, 128), jnp.float32), pltpu.VMEM((block, offs * ch), jnp.bfloat16)],
        compiler_params=pltpu.CompilerParams(vmem_limit_bytes=56 << 20),
    )(idx, left, own, right, w, lin)

def gather_rows(near, block):
    rows, offs = near.shape
    h = jnp.arange(rows, dtype=jnp.int32)[:, None]
    idx = 2 * jnp.where(near < 0, 3 * rows, near + h)
    return idx.reshape(rows // block, block, offs).transpose(0, 2, 1).reshape(rows // block, 1, offs * block)


def on_device(
    points,
    qkv_one,
    proj_one,
    up_one,
    down_one,
    hilbert_device,
    hilbert_position,
    neighbors,
    conv_two,
    linear_two,
):
    row_count = points.shape[0]
    channels = points.shape[1]
    half_patch = PATCH // 2
    normed = layer_norm(points).astype(jnp.bfloat16)
    projected = jnp.dot(normed, qkv_one, preferred_element_type=jnp.float32).astype(jnp.bfloat16)
    extended = with_halo(projected[:, channels:], ((("curve", "group"), 0),), half_patch, True)
    mixed = block_attention(projected[:, :channels], extended[:, :channels], extended[:, channels:])
    z_out = finish(points, mixed, proj_one, up_one, down_one)
    devices = lax.axis_size(("curve", "group"))
    capacity = 2 * row_count // devices
    onehot = (hilbert_device[:, None] == jnp.arange(devices, dtype=jnp.int32)[None, :]).astype(
        jnp.int32
    )
    running = jnp.cumsum(onehot, axis=0)
    slot_index = jnp.sum(onehot * running, axis=1) - 1
    send_index = hilbert_device * capacity + slot_index
    send_rows = jnp.zeros((devices * capacity, channels), jnp.bfloat16).at[send_index].set(z_out)
    send_place = jnp.full((devices * capacity,), -1, jnp.int32).at[send_index].set(hilbert_position)
    got_rows, got_place = (
        lax.all_to_all(
            send_rows.reshape(devices, capacity, channels),
            ("curve", "group"),
            split_axis=0,
            concat_axis=0,
            tiled=True,
        ),
        lax.all_to_all(
            send_place.reshape(devices, capacity),
            ("curve", "group"),
            split_axis=0,
            concat_axis=0,
            tiled=True,
        ),
    )
    flat_place = got_place.reshape(-1)
    target = jnp.where(flat_place < 0, row_count, flat_place)
    serial = (
        jnp.zeros((row_count, channels), jnp.bfloat16)
        .at[target]
        .set(got_rows.reshape(-1, channels), mode="drop")
    )
    axes = ("curve", "group")
    ups = [(i, i + 1) for i in range(devices - 1)]
    downs = [(i + 1, i) for i in range(devices - 1)]
    left = lax.ppermute(serial, axes, ups)
    right = lax.ppermute(serial, axes, downs)
    block = min(512, row_count)
    return position_conv(gather_rows(neighbors, block), left, serial, right, conv_two, linear_two, block)


def solution(mesh):
    return jax.shard_map(
        on_device,
        mesh=mesh,
        in_specs=(
            P(("curve", "group"), None),
            P(),
            P(),
            P(),
            P(),
            P(("curve", "group")),
            P(("curve", "group")),
            P(("curve", "group"), None),
            P(),
            P(),
        ),
        out_specs=P(("curve", "group"), None),
        check_vma=False,
    )
```

```python
import functools

import jax
import jax.numpy as jnp
from jax import lax
from jax.experimental import pallas as pl
from jax.experimental.pallas import tpu as pltpu
from jax.sharding import PartitionSpec as P

HEADS = 16
HEAD_DIM = 16
PATCH = 1024
LANES = 128
EPS = 1e-05
LOG2E = 1.4426950408889634
AXES = ("curve", "group")


def layer_norm(values):
    values = values.astype(jnp.float32)
    center = jnp.mean(values, axis=-1, keepdims=True)
    offset = values - center
    spread = jnp.mean(offset * offset, axis=-1, keepdims=True)
    return offset * lax.rsqrt(spread + EPS)


def dot(left, right):
    return jnp.dot(left, right, preferred_element_type=jnp.float32)


def gelu(values):
    return 0.5 * values * (1.0 + lax.erf(values * 0.7071067811865476))


def slots_kernel(devices, capacity, device_ref, position_ref, index_ref, place_ref):
    rows = device_ref.shape[1]
    chunk = min(256, rows)
    row_id = lax.broadcasted_iota(jnp.int32, (chunk, chunk), 0)
    col_id = lax.broadcasted_iota(jnp.int32, (chunk, chunk), 1)
    before = (row_id <= col_id).astype(jnp.float32).astype(jnp.bfloat16)
    device_id = lax.broadcasted_iota(jnp.int32, (devices, chunk), 0)
    slot_id = lax.broadcasted_iota(jnp.int32, (capacity, chunk), 0)
    carry = jnp.zeros((devices, 1), jnp.float32)
    place = jnp.zeros((2 * devices, capacity), jnp.float32)
    for part in range(rows // chunk):
        span = slice(part * chunk, (part + 1) * chunk)
        target = device_ref[:, span]
        mine = (device_id == target).astype(jnp.float32)
        running = dot(mine.astype(jnp.bfloat16), before) + carry
        carry = running[:, chunk - 1 : chunk]
        slot = (jnp.sum(mine * running, axis=0, keepdims=True) - 1.0).astype(jnp.int32)
        index_ref[:, span] = 2 * (target * capacity + slot)
        code = position_ref[:, span] + 1
        high = mine * (code // LANES).astype(jnp.float32)
        low = mine * (code % LANES).astype(jnp.float32)
        here = (slot_id == slot).astype(jnp.float32).astype(jnp.bfloat16)
        place += lax.dot_general(
            jnp.concatenate([high, low], axis=0).astype(jnp.bfloat16),
            here,
            (((1,), (1,)), ((), ())),
            preferred_element_type=jnp.float32,
        )
    place_ref[...] = 2 * (place[:devices] * float(LANES) + place[devices:]).astype(jnp.int32)


def find_slots(device, position, devices, capacity):
    rows = device.shape[0]
    return pl.pallas_call(
        functools.partial(slots_kernel, devices, capacity),
        out_shape=(
            jax.ShapeDtypeStruct((1, rows), jnp.int32),
            jax.ShapeDtypeStruct((devices, capacity), jnp.int32),
        ),
        name="find_slots",
    )(device.reshape(1, rows), position.reshape(1, rows))


def block_kernel(
    index_ref,
    left_ref,
    own_ref,
    right_ref,
    qkv_ref,
    proj_ref,
    up_ref,
    down_ref,
    send_ref,
    query,
    key,
    value,
    pairs,
    table,
):
    step = pl.program_id(0)
    rows, channels = own_ref.shape
    half = PATCH // 2

    @pl.when(step == 0)
    def _():
        count = rows // half
        for part in range(count + 2):
            if part == 0:
                source = left_ref[...]
            elif part == count + 1:
                source = right_ref[...]
            else:
                source = own_ref[(part - 1) * half : part * half, :]
            normed = layer_norm(source).astype(jnp.bfloat16)
            span = slice(part * half, (part + 1) * half)
            key[:, span] = lax.dot_general(
                qkv_ref[:, channels : 2 * channels],
                normed,
                (((0,), (1,)), ((), ())),
                preferred_element_type=jnp.float32,
            ).astype(jnp.bfloat16)
            value[span, :] = dot(normed, qkv_ref[:, 2 * channels :]).astype(jnp.bfloat16)
            if 0 < part <= count:
                query[(part - 1) * half : part * half, :] = dot(normed, qkv_ref[:, :channels]).astype(jnp.bfloat16)

    first = pl.multiple_of(step * half, half)
    start = pl.multiple_of(PATCH * ((step + 1) // 2), PATCH)
    per_group = LANES // HEAD_DIM
    head_of = lax.broadcasted_iota(jnp.int32, (1, LANES), 1) // HEAD_DIM
    scale = HEAD_DIM ** (-0.5) * LOG2E
    pieces = []
    for group in range(channels // LANES):
        lanes = slice(group * LANES, (group + 1) * LANES)
        queries = query[pl.ds(first, half), lanes]
        keys = key[lanes, pl.ds(start, PATCH)]
        values = value[pl.ds(start, PATCH), lanes]
        total = None
        for head in range(per_group):
            mine = head_of == head
            scores = dot(jnp.where(mine, queries, jnp.zeros_like(queries)), keys)
            peak = jnp.max(scores, axis=1, keepdims=True)
            weights = jnp.exp2((scores - peak) * scale).astype(jnp.bfloat16)
            ones = jnp.broadcast_to(mine.astype(jnp.float32).astype(jnp.bfloat16), values.shape)
            both = jnp.concatenate([jnp.where(mine, values, jnp.zeros_like(values)), ones], axis=1)
            result = dot(weights, both)
            total = result if total is None else total + result
        pieces.append((total[:, :LANES] / total[:, LANES:]).astype(jnp.bfloat16))
    mixed = jnp.concatenate(pieces, axis=1)
    after = (own_ref[pl.ds(first, half), :].astype(jnp.float32) + dot(mixed, proj_ref[...])).astype(jnp.bfloat16)
    normed = layer_norm(after).astype(jnp.bfloat16)
    hidden = gelu(dot(normed, up_ref[...])).astype(jnp.bfloat16)
    out = (after.astype(jnp.float32) + dot(hidden, down_ref[...])).astype(jnp.bfloat16).astype(jnp.float32)
    pairs[pl.ds(0, half, stride=2), :] = out[:, :LANES]
    pairs[pl.ds(1, half, stride=2), :] = out[:, LANES:]
    for row in range(half):
        slot = pl.multiple_of(index_ref[0, first + row], 2)
        table[pl.ds(slot, 2), :] = pairs[2 * row : 2 * row + 2, :]

    @pl.when(step == pl.num_programs(0) - 1)
    def _():
        slots = send_ref.shape[0]
        for side in range(2):
            send_ref[:, side * LANES : (side + 1) * LANES] = table[pl.ds(side, slots, stride=2), :].astype(jnp.bfloat16)


def block_one(index, left, own, right, qkv, proj, up, down, slots):
    rows, channels = own.shape
    half = PATCH // 2
    vmem = pl.BlockSpec(memory_space=pltpu.VMEM)
    return pl.pallas_call(
        block_kernel,
        out_shape=jax.ShapeDtypeStruct((slots, channels), jnp.bfloat16),
        grid=(rows // half,),
        in_specs=[pl.BlockSpec(memory_space=pltpu.SMEM)] + [vmem] * 7,
        out_specs=vmem,
        scratch_shapes=[
            pltpu.VMEM((rows, channels), jnp.bfloat16),
            pltpu.VMEM((channels, rows + PATCH), jnp.bfloat16),
            pltpu.VMEM((rows + PATCH, channels), jnp.bfloat16),
            pltpu.VMEM((2 * half, LANES), jnp.float32),
            pltpu.VMEM((2 * slots, LANES), jnp.float32),
        ],
        compiler_params=pltpu.CompilerParams(vmem_limit_bytes=56 << 20),
        name="block_one",
    )(index, left, own, right, qkv, proj, up, down)


def settle_kernel(place_ref, got_ref, serial_ref, pairs, table):
    slots = got_ref.shape[0]
    rows = serial_ref.shape[0]
    capacity = place_ref.shape[1]
    for side in range(2):
        pairs[pl.ds(side, slots, stride=2), :] = got_ref[:, side * LANES : (side + 1) * LANES].astype(jnp.float32)

    def body(source, carry):
        base = pl.multiple_of(source * (2 * capacity), 2 * capacity)
        for slot in range(capacity):
            target = pl.multiple_of(place_ref[source, slot] + 6, 2)
            table[pl.ds(target, 2), :] = pairs[pl.ds(base + 2 * slot, 2), :]
        return carry

    lax.fori_loop(0, place_ref.shape[0], body, 0)
    for side in range(2):
        serial_ref[:, side * LANES : (side + 1) * LANES] = table[pl.ds(8 + side, rows, stride=2), :].astype(
            jnp.bfloat16
        )


def settle(place, got, rows):
    slots, channels = got.shape
    vmem = pl.BlockSpec(memory_space=pltpu.VMEM)
    return pl.pallas_call(
        settle_kernel,
        out_shape=jax.ShapeDtypeStruct((rows, channels), jnp.bfloat16),
        in_specs=[pl.BlockSpec(memory_space=pltpu.SMEM), vmem],
        out_specs=vmem,
        scratch_shapes=[pltpu.VMEM((2 * slots, LANES), jnp.float32), pltpu.VMEM((2 * rows + 8, LANES), jnp.float32)],
        compiler_params=pltpu.CompilerParams(vmem_limit_bytes=56 << 20),
        name="settle",
    )(place, got)


def conv_kernel(block, offs, rows, idx_ref, left_ref, own_ref, right_ref, w_ref, lin_ref, out_ref, tab, buf, lhs):
    step = pl.program_id(0)
    lanes = LANES

    @pl.when(step == 0)
    def _():
        for part, ref in enumerate((left_ref, own_ref, right_ref)):
            for half in range(2):
                tab[pl.ds(2 * part * rows + half, rows, stride=2), :] = ref[:, half * lanes:(half + 1) * lanes].astype(jnp.float32)
        tab[pl.ds(6 * rows, 8), :] = jnp.zeros((8, lanes), jnp.float32)

    start = pl.multiple_of(step * block, block)
    width = 2 * lanes
    mid = offs // 2
    for k, ref in ((0, left_ref), (mid, own_ref), (offs - 1, right_ref)):
        lhs[:, k * width:(k + 1) * width] = ref[pl.ds(start, block), :]

    def one(o):
        base = o * block
        for j in range(block):
            buf[2 * j:2 * j + 2, :] = tab[pl.ds(pl.multiple_of(idx_ref[0, 0, base + j], 2), 2), :]
        for half in range(2):
            lhs[:, pl.ds(pl.multiple_of(o * width + half * lanes, lanes), lanes)] = buf[pl.ds(half, block, stride=2), :].astype(jnp.bfloat16)

    def body(o, carry):
        one(o)
        return carry
    lax.fori_loop(1, mid, body, 0)
    lax.fori_loop(mid + 1, offs - 1, body, 0)
    conv = jnp.dot(lhs[...], w_ref[...], preferred_element_type=jnp.float32).astype(jnp.bfloat16)
    linear = jnp.dot(conv, lin_ref[...], preferred_element_type=jnp.float32)
    out_ref[...] = (own_ref[pl.ds(start, block), :].astype(jnp.float32) + layer_norm(linear)).astype(jnp.bfloat16)

def position_conv(idx, left, own, right, w, lin, block):
    rows, ch = own.shape
    offs = w.shape[0] // ch
    vm = pl.BlockSpec(memory_space=pltpu.VMEM)
    return pl.pallas_call(
        functools.partial(conv_kernel, block, offs, rows),
        out_shape=jax.ShapeDtypeStruct((rows, ch), jnp.bfloat16),
        grid=(rows // block,),
        in_specs=[pl.BlockSpec((1, 1, offs * block), lambda i: (i, 0, 0), memory_space=pltpu.SMEM), vm, vm, vm, vm, vm],
        out_specs=pl.BlockSpec((block, ch), lambda i: (i, 0)),
        scratch_shapes=[pltpu.VMEM((6 * rows + 8, LANES), jnp.float32), pltpu.VMEM((2 * block, LANES), jnp.float32), pltpu.VMEM((block, offs * ch), jnp.bfloat16)],
        compiler_params=pltpu.CompilerParams(vmem_limit_bytes=56 << 20),
    )(idx, left, own, right, w, lin)

def gather_rows(near, block):
    rows, offs = near.shape
    h = jnp.arange(rows, dtype=jnp.int32)[:, None]
    idx = 2 * jnp.where(near < 0, 3 * rows, near + h)
    return idx.reshape(rows // block, block, offs).transpose(0, 2, 1).reshape(rows // block, 1, offs * block)


def on_device(
    points,
    qkv_one,
    proj_one,
    up_one,
    down_one,
    hilbert_device,
    hilbert_position,
    neighbors,
    conv_two,
    linear_two,
):
    row_count, channels = points.shape
    half = PATCH // 2
    devices = lax.axis_size(AXES)
    capacity = 2 * row_count // devices
    ring_up = [(i, (i + 1) % devices) for i in range(devices)]
    ring_down = [((i + 1) % devices, i) for i in range(devices)]
    before = lax.ppermute(points[row_count - half :], AXES, ring_up)
    behind = lax.ppermute(points[:half], AXES, ring_down)
    index, place = find_slots(hilbert_device, hilbert_position, devices, capacity)
    got_place = lax.all_to_all(place, AXES, split_axis=0, concat_axis=0, tiled=True)
    send = block_one(index, before, points, behind, qkv_one, proj_one, up_one, down_one, devices * capacity)
    got = lax.all_to_all(
        send.reshape(devices, capacity, channels), AXES, split_axis=0, concat_axis=0, tiled=True
    )
    serial = settle(got_place, got.reshape(devices * capacity, channels), row_count)
    left = lax.ppermute(serial, AXES, ring_up[:-1])
    right = lax.ppermute(serial, AXES, ring_down[:-1])
    block = min(512, row_count)
    return position_conv(gather_rows(neighbors, block), left, serial, right, conv_two, linear_two, block)


def solution(mesh):
    split = P(AXES)
    rows = P(AXES, None)
    return jax.shard_map(
        on_device,
        mesh=mesh,
        in_specs=(rows, P(), P(), P(), P(), split, split, rows, P(), P()),
        out_specs=rows,
        check_vma=False,
    )
```

```python
import functools

import jax
import jax.numpy as jnp
from jax import lax
from jax.experimental import pallas as pl
from jax.experimental.pallas import tpu as pltpu
from jax.sharding import PartitionSpec as P

HEADS = 16
HEAD_DIM = 16
PATCH = 1024
LANES = 128
EPS = 1e-05
LOG2E = 1.4426950408889634
AXES = ("curve", "group")


def layer_norm(values):
    values = values.astype(jnp.float32)
    center = jnp.mean(values, axis=-1, keepdims=True)
    offset = values - center
    spread = jnp.mean(offset * offset, axis=-1, keepdims=True)
    return offset * lax.rsqrt(spread + EPS)


def dot(left, right):
    return jnp.dot(left, right, preferred_element_type=jnp.float32)


def gelu(values):
    return 0.5 * values * (1.0 + lax.erf(values * 0.7071067811865476))


def slots_kernel(devices, capacity, device_ref, position_ref, index_ref, place_ref):
    rows = device_ref.shape[1]
    chunk = min(256, rows)
    row_id = lax.broadcasted_iota(jnp.int32, (chunk, chunk), 0)
    col_id = lax.broadcasted_iota(jnp.int32, (chunk, chunk), 1)
    before = (row_id <= col_id).astype(jnp.float32).astype(jnp.bfloat16)
    device_id = lax.broadcasted_iota(jnp.int32, (devices, chunk), 0)
    slot_id = lax.broadcasted_iota(jnp.int32, (capacity, chunk), 0)
    carry = jnp.zeros((devices, 1), jnp.float32)
    place = jnp.zeros((2 * devices, capacity), jnp.float32)
    for part in range(rows // chunk):
        span = slice(part * chunk, (part + 1) * chunk)
        target = device_ref[:, span]
        mine = (device_id == target).astype(jnp.float32)
        running = dot(mine.astype(jnp.bfloat16), before) + carry
        carry = running[:, chunk - 1 : chunk]
        slot = (jnp.sum(mine * running, axis=0, keepdims=True) - 1.0).astype(jnp.int32)
        index_ref[:, span] = 2 * (target * capacity + slot)
        code = position_ref[:, span] + 1
        high = mine * (code // LANES).astype(jnp.float32)
        low = mine * (code % LANES).astype(jnp.float32)
        here = (slot_id == slot).astype(jnp.float32).astype(jnp.bfloat16)
        place += lax.dot_general(
            jnp.concatenate([high, low], axis=0).astype(jnp.bfloat16),
            here,
            (((1,), (1,)), ((), ())),
            preferred_element_type=jnp.float32,
        )
    place_ref[...] = 2 * (place[:devices] * float(LANES) + place[devices:]).astype(jnp.int32)


def find_slots(device, position, devices, capacity):
    rows = device.shape[0]
    return pl.pallas_call(
        functools.partial(slots_kernel, devices, capacity),
        out_shape=(
            jax.ShapeDtypeStruct((1, rows), jnp.int32),
            jax.ShapeDtypeStruct((devices, capacity), jnp.int32),
        ),
        name="find_slots",
    )(device.reshape(1, rows), position.reshape(1, rows))


def block_kernel(
    index_ref,
    left_ref,
    own_ref,
    right_ref,
    qkv_ref,
    proj_ref,
    up_ref,
    down_ref,
    send_ref,
    query,
    key,
    value,
    pairs,
    table,
):
    step = pl.program_id(0)
    rows, channels = own_ref.shape
    half = PATCH // 2

    @pl.when(step == 0)
    def _():
        count = rows // half
        for part in range(count + 2):
            if part == 0:
                source = left_ref[...]
            elif part == count + 1:
                source = right_ref[...]
            else:
                source = own_ref[(part - 1) * half : part * half, :]
            normed = layer_norm(source).astype(jnp.bfloat16)
            span = slice(part * half, (part + 1) * half)
            key[:, span] = lax.dot_general(
                qkv_ref[:, channels : 2 * channels],
                normed,
                (((0,), (1,)), ((), ())),
                preferred_element_type=jnp.float32,
            ).astype(jnp.bfloat16)
            value[span, :] = dot(normed, qkv_ref[:, 2 * channels :]).astype(jnp.bfloat16)
            if 0 < part <= count:
                query[(part - 1) * half : part * half, :] = dot(normed, qkv_ref[:, :channels]).astype(jnp.bfloat16)

    first = pl.multiple_of(step * half, half)
    start = pl.multiple_of(PATCH * ((step + 1) // 2), PATCH)
    per_group = LANES // HEAD_DIM
    head_of = lax.broadcasted_iota(jnp.int32, (1, LANES), 1) // HEAD_DIM
    scale = HEAD_DIM ** (-0.5) * LOG2E
    pieces = []
    for group in range(channels // LANES):
        lanes = slice(group * LANES, (group + 1) * LANES)
        queries = query[pl.ds(first, half), lanes]
        keys = key[lanes, pl.ds(start, PATCH)]
        values = value[pl.ds(start, PATCH), lanes]
        total = None
        for head in range(per_group):
            mine = head_of == head
            scores = dot(jnp.where(mine, queries, jnp.zeros_like(queries)), keys)
            peak = jnp.max(scores, axis=1, keepdims=True)
            weights = jnp.exp2((scores - peak) * scale).astype(jnp.bfloat16)
            ones = jnp.broadcast_to(mine.astype(jnp.float32).astype(jnp.bfloat16), values.shape)
            both = jnp.concatenate([jnp.where(mine, values, jnp.zeros_like(values)), ones], axis=1)
            result = dot(weights, both)
            total = result if total is None else total + result
        pieces.append((total[:, :LANES] / total[:, LANES:]).astype(jnp.bfloat16))
    mixed = jnp.concatenate(pieces, axis=1)
    after = (own_ref[pl.ds(first, half), :].astype(jnp.float32) + dot(mixed, proj_ref[...])).astype(jnp.bfloat16)
    normed = layer_norm(after).astype(jnp.bfloat16)
    hidden = gelu(dot(normed, up_ref[...])).astype(jnp.bfloat16)
    out = (after.astype(jnp.float32) + dot(hidden, down_ref[...])).astype(jnp.bfloat16).astype(jnp.float32)
    pairs[pl.ds(0, half, stride=2), :] = out[:, :LANES]
    pairs[pl.ds(1, half, stride=2), :] = out[:, LANES:]
    for row in range(half):
        slot = pl.multiple_of(index_ref[0, first + row], 2)
        table[pl.ds(slot, 2), :] = pairs[2 * row : 2 * row + 2, :]

    @pl.when(step == pl.num_programs(0) - 1)
    def _():
        slots = send_ref.shape[0]
        for side in range(2):
            send_ref[:, side * LANES : (side + 1) * LANES] = table[pl.ds(side, slots, stride=2), :].astype(jnp.bfloat16)


def block_one(index, left, own, right, qkv, proj, up, down, slots):
    rows, channels = own.shape
    half = PATCH // 2
    vmem = pl.BlockSpec(memory_space=pltpu.VMEM)
    return pl.pallas_call(
        block_kernel,
        out_shape=jax.ShapeDtypeStruct((slots, channels), jnp.bfloat16),
        grid=(rows // half,),
        in_specs=[pl.BlockSpec(memory_space=pltpu.SMEM)] + [vmem] * 7,
        out_specs=vmem,
        scratch_shapes=[
            pltpu.VMEM((rows, channels), jnp.bfloat16),
            pltpu.VMEM((channels, rows + PATCH), jnp.bfloat16),
            pltpu.VMEM((rows + PATCH, channels), jnp.bfloat16),
            pltpu.VMEM((2 * half, LANES), jnp.float32),
            pltpu.VMEM((2 * slots, LANES), jnp.float32),
        ],
        compiler_params=pltpu.CompilerParams(vmem_limit_bytes=56 << 20),
        name="block_one",
    )(index, left, own, right, qkv, proj, up, down)


def settle_kernel(place_ref, got_ref, serial_ref, pairs, table):
    slots = got_ref.shape[0]
    rows = serial_ref.shape[0]
    capacity = place_ref.shape[1]
    for side in range(2):
        pairs[pl.ds(side, slots, stride=2), :] = got_ref[:, side * LANES : (side + 1) * LANES].astype(jnp.float32)

    def body(source, carry):
        base = pl.multiple_of(source * (2 * capacity), 2 * capacity)
        for slot in range(capacity):
            target = pl.multiple_of(place_ref[source, slot] + 6, 2)
            table[pl.ds(target, 2), :] = pairs[pl.ds(base + 2 * slot, 2), :]
        return carry

    lax.fori_loop(0, place_ref.shape[0], body, 0)
    for side in range(2):
        serial_ref[:, side * LANES : (side + 1) * LANES] = table[pl.ds(8 + side, rows, stride=2), :].astype(
            jnp.bfloat16
        )


def settle(place, got, rows):
    slots, channels = got.shape
    vmem = pl.BlockSpec(memory_space=pltpu.VMEM)
    return pl.pallas_call(
        settle_kernel,
        out_shape=jax.ShapeDtypeStruct((rows, channels), jnp.bfloat16),
        in_specs=[pl.BlockSpec(memory_space=pltpu.SMEM), vmem],
        out_specs=vmem,
        scratch_shapes=[pltpu.VMEM((2 * slots, LANES), jnp.float32), pltpu.VMEM((2 * rows + 8, LANES), jnp.float32)],
        compiler_params=pltpu.CompilerParams(vmem_limit_bytes=56 << 20),
        name="settle",
    )(place, got)


CHUNK = 32


def pick(step, values):
    return sum(jnp.where(step == place, value, 0) for place, value in enumerate(values) if value)


def conv_kernel(segment, starts, stores, sources, kept, rows, index_ref, *refs):
    parts, refs = refs[: len(sources)], refs[len(sources) :]
    olds, refs = refs[: len(kept)], refs[len(kept) :]
    weight_ref, linear_ref, out_ref, table, ping, pong, operand = refs
    step = pl.program_id(0)
    width = out_ref.shape[1]
    offsets = weight_ref.shape[0] // width
    middle = offsets // 2
    moved = offsets - 3
    block = 2 * segment
    sides = width // LANES

    @pl.when(step == 0)
    def _():
        for (first, count), ref in zip(sources, parts):
            for side in range(sides):
                table[pl.ds(2 * first + side, count, stride=2), :] = ref[:, side * LANES : (side + 1) * LANES].astype(
                    jnp.float32
                )
        table[pl.ds(6 * rows, 8), :] = jnp.zeros((8, LANES), jnp.float32)
        for first, ref in zip(kept, olds):
            out_ref[first : first + ref.shape[0], :] = ref[...]

    begins = [pl.multiple_of(pick(step, [pair[piece] for pair in starts]), segment) for piece in range(2)]
    ends = [pl.multiple_of(pick(step, [pair[piece] for pair in stores]), segment) for piece in range(2)]
    for span, offset in enumerate((0, middle, offsets - 1)):
        for piece, begin in enumerate(begins):
            for side in range(sides):
                operand[
                    piece * segment : (piece + 1) * segment,
                    offset * width + side * LANES : offset * width + (side + 1) * LANES,
                ] = table[pl.ds(2 * (span * rows + begin) + side, segment, stride=2), :].astype(jnp.bfloat16)

    def fetch(order, buffer, row):
        for other in range(row, row + CHUNK):
            source = pl.multiple_of(index_ref[0, 0, order * block + other], 2)
            buffer[2 * other : 2 * other + 2, :] = table[pl.ds(source, 2), :]

    def settle_columns(order, buffer, row):
        offset = order + jnp.where(order < middle - 1, 1, 2)
        column = pl.multiple_of(offset * width, width)
        halves = [buffer[pl.ds(2 * row + side, CHUNK, stride=2), :].astype(jnp.bfloat16) for side in range(sides)]
        operand[row : row + CHUNK, pl.ds(column, width)] = jnp.concatenate(halves, axis=1)

    def body(pair, carry):
        for turn, (filled, other) in enumerate(((ping, pong), (pong, ping))):
            order = 2 * pair + turn
            for row in range(0, block, CHUNK):
                fetch(order, filled, row)
                settle_columns(jnp.maximum(order - 1, 0), other, row)
        return carry

    lax.fori_loop(0, moved // 2, body, 0)
    for row in range(0, block, CHUNK):
        settle_columns(jnp.int32(moved - 1), pong, row)
    conv = dot(operand[...], weight_ref[...]).astype(jnp.bfloat16)
    normed = layer_norm(dot(conv, linear_ref[...]))
    for piece in range(2):
        begin = 2 * (rows + begins[piece])
        own = [table[pl.ds(begin + side, segment, stride=2), :] for side in range(sides)]
        result = jnp.concatenate(own, axis=1) + normed[piece * segment : (piece + 1) * segment]
        out_ref[pl.ds(ends[piece], segment), :] = result.astype(jnp.bfloat16)


def position_conv(near, starts, stores, count, sources, parts, kept, olds, weight, linear):
    rows, offsets = near.shape
    channels = linear.shape[0]
    segment = rows // 8
    middle = offsets // 2
    steps = len(starts)
    row_id = jnp.arange(rows, dtype=jnp.int32)[:, None]
    index = 2 * jnp.where(near < 0, 3 * rows, near + row_id)
    index = jnp.concatenate([index[:, 1:middle], index[:, middle + 1 : offsets - 1]], axis=1)
    index = jnp.concatenate([index[begin : begin + segment] for pair in starts for begin in pair], axis=0)
    index = index.reshape(steps, 2 * segment, offsets - 3).transpose(0, 2, 1).reshape(steps, 1, -1)
    vmem = pl.BlockSpec(memory_space=pltpu.VMEM)
    return pl.pallas_call(
        functools.partial(conv_kernel, segment, starts, stores, sources, kept, rows),
        out_shape=jax.ShapeDtypeStruct((count, channels), jnp.bfloat16),
        grid=(steps,),
        in_specs=[pl.BlockSpec((1, 1, index.shape[2]), lambda step: (step, 0, 0), memory_space=pltpu.SMEM)]
        + [vmem] * (len(parts) + len(olds) + 2),
        out_specs=vmem,
        scratch_shapes=[
            pltpu.VMEM((6 * rows + 8, LANES), jnp.float32),
            pltpu.VMEM((4 * segment, LANES), jnp.float32),
            pltpu.VMEM((4 * segment, LANES), jnp.float32),
            pltpu.VMEM((2 * segment, offsets * channels), jnp.bfloat16),
        ],
        compiler_params=pltpu.CompilerParams(vmem_limit_bytes=56 << 20),
        name="position_conv",
    )(index, *parts, *olds, weight, linear)


def on_device(
    points,
    qkv_one,
    proj_one,
    up_one,
    down_one,
    hilbert_device,
    hilbert_position,
    neighbors,
    conv_two,
    linear_two,
):
    row_count, channels = points.shape
    half = PATCH // 2
    devices = lax.axis_size(AXES)
    capacity = 2 * row_count // devices
    ring_up = [(i, (i + 1) % devices) for i in range(devices)]
    ring_down = [((i + 1) % devices, i) for i in range(devices)]
    before = lax.ppermute(points[row_count - half :], AXES, ring_up)
    behind = lax.ppermute(points[:half], AXES, ring_down)
    index, place = find_slots(hilbert_device, hilbert_position, devices, capacity)
    got_place = lax.all_to_all(place, AXES, split_axis=0, concat_axis=0, tiled=True)
    send = block_one(index, before, points, behind, qkv_one, proj_one, up_one, down_one, devices * capacity)
    got = lax.all_to_all(
        send.reshape(devices, capacity, channels), AXES, split_axis=0, concat_axis=0, tiled=True
    )
    serial = settle(got_place, got.reshape(devices * capacity, channels), row_count)
    segment = row_count // 8
    low, high = 3 * segment, 5 * segment
    left_near = lax.ppermute(serial[low:], AXES, ring_up[:-1])
    right_near = lax.ppermute(serial[:high], AXES, ring_down[:-1])
    left_far = lax.ppermute(serial[:low], AXES, ring_up[:-1])
    right_far = lax.ppermute(serial[high:], AXES, ring_down[:-1])
    parts = [left_near, serial, right_near]
    sources = [(low, row_count - low), (row_count, row_count), (2 * row_count, high)]
    inner = [(low, low + segment)]
    outer = [(0, segment), (2 * segment, high), (6 * segment, 7 * segment)]
    center = position_conv(
        neighbors, inner, [(0, segment)], 2 * segment, sources, parts, [], [], conv_two, linear_two
    )
    parts += [left_far, right_far]
    sources += [(0, low), (2 * row_count + high, row_count - high)]
    return position_conv(
        neighbors, outer, outer, row_count, sources, parts, [low], [center], conv_two, linear_two
    )


def solution(mesh):
    split = P(AXES)
    rows = P(AXES, None)
    return jax.shard_map(
        on_device,
        mesh=mesh,
        in_specs=(rows, P(), P(), P(), P(), split, split, rows, P(), P()),
        out_specs=rows,
        check_vma=False,
    )
```

```python
import functools

import jax
import jax.numpy as jnp
from jax import lax
from jax.experimental import pallas as pl
from jax.experimental.pallas import tpu as pltpu
from jax.sharding import PartitionSpec as P

HEADS = 16
HEAD_DIM = 16
PATCH = 1024
LANES = 128
EPS = 1e-05
LOG2E = 1.4426950408889634
AXES = ("curve", "group")


def layer_norm(values):
    values = values.astype(jnp.float32)
    center = jnp.mean(values, axis=-1, keepdims=True)
    offset = values - center
    spread = jnp.mean(offset * offset, axis=-1, keepdims=True)
    return offset * lax.rsqrt(spread + EPS)


def dot(left, right):
    return jnp.dot(left, right, preferred_element_type=jnp.float32)


def gelu(values):
    return 0.5 * values * (1.0 + lax.erf(values * 0.7071067811865476))


def slots_kernel(devices, capacity, device_ref, position_ref, index_ref, place_ref):
    rows = device_ref.shape[1]
    chunk = min(256, rows)
    row_id = lax.broadcasted_iota(jnp.int32, (chunk, chunk), 0)
    col_id = lax.broadcasted_iota(jnp.int32, (chunk, chunk), 1)
    before = (row_id <= col_id).astype(jnp.float32).astype(jnp.bfloat16)
    device_id = lax.broadcasted_iota(jnp.int32, (devices, chunk), 0)
    slot_id = lax.broadcasted_iota(jnp.int32, (capacity, chunk), 0)
    carry = jnp.zeros((devices, 1), jnp.float32)
    place = jnp.zeros((2 * devices, capacity), jnp.float32)
    for part in range(rows // chunk):
        span = slice(part * chunk, (part + 1) * chunk)
        target = device_ref[:, span]
        mine = (device_id == target).astype(jnp.float32)
        running = dot(mine.astype(jnp.bfloat16), before) + carry
        carry = running[:, chunk - 1 : chunk]
        slot = (jnp.sum(mine * running, axis=0, keepdims=True) - 1.0).astype(jnp.int32)
        index_ref[:, span] = 2 * (target * capacity + slot)
        code = position_ref[:, span] + 1
        high = mine * (code // LANES).astype(jnp.float32)
        low = mine * (code % LANES).astype(jnp.float32)
        here = (slot_id == slot).astype(jnp.float32).astype(jnp.bfloat16)
        place += lax.dot_general(
            jnp.concatenate([high, low], axis=0).astype(jnp.bfloat16),
            here,
            (((1,), (1,)), ((), ())),
            preferred_element_type=jnp.float32,
        )
    place_ref[...] = 2 * (place[:devices] * float(LANES) + place[devices:]).astype(jnp.int32)


def find_slots(device, position, devices, capacity):
    rows = device.shape[0]
    return pl.pallas_call(
        functools.partial(slots_kernel, devices, capacity),
        out_shape=(
            jax.ShapeDtypeStruct((1, rows), jnp.int32),
            jax.ShapeDtypeStruct((devices, capacity), jnp.int32),
        ),
        name="find_slots",
    )(device.reshape(1, rows), position.reshape(1, rows))


def project(source, key, value, weight_ref, key_ref, value_ref, query_ref=None, query=0):
    count, channels = source.shape
    normed = layer_norm(source).astype(jnp.bfloat16)
    key_ref[:, key : key + count] = lax.dot_general(
        weight_ref[:, channels : 2 * channels],
        normed,
        (((0,), (1,)), ((), ())),
        preferred_element_type=jnp.float32,
    ).astype(jnp.bfloat16)
    value_ref[value : value + count, :] = dot(normed, weight_ref[:, 2 * channels :]).astype(jnp.bfloat16)
    if query_ref is not None:
        query_ref[query : query + count, :] = dot(normed, weight_ref[:, :channels]).astype(jnp.bfloat16)


def transform(residual, first, start, query, key, value, proj_ref, up_ref, down_ref):
    half, channels = residual.shape
    per_group = LANES // HEAD_DIM
    head_of = lax.broadcasted_iota(jnp.int32, (1, LANES), 1) // HEAD_DIM
    scale = HEAD_DIM ** (-0.5) * LOG2E
    pieces = []
    for group in range(channels // LANES):
        lanes = slice(group * LANES, (group + 1) * LANES)
        queries = query[pl.ds(first, half), lanes]
        keys = key[lanes, pl.ds(start, PATCH)]
        values = value[pl.ds(start, PATCH), lanes]
        total = None
        for head in range(per_group):
            mine = head_of == head
            scores = dot(jnp.where(mine, queries, jnp.zeros_like(queries)), keys)
            peak = jnp.max(scores, axis=1, keepdims=True)
            weights = jnp.exp2((scores - peak) * scale).astype(jnp.bfloat16)
            ones = jnp.broadcast_to(mine.astype(jnp.float32).astype(jnp.bfloat16), values.shape)
            both = jnp.concatenate([jnp.where(mine, values, jnp.zeros_like(values)), ones], axis=1)
            result = dot(weights, both)
            total = result if total is None else total + result
        pieces.append((total[:, :LANES] / total[:, LANES:]).astype(jnp.bfloat16))
    mixed = jnp.concatenate(pieces, axis=1)
    after = (residual.astype(jnp.float32) + dot(mixed, proj_ref[...])).astype(jnp.bfloat16)
    normed = layer_norm(after).astype(jnp.bfloat16)
    hidden = gelu(dot(normed, up_ref[...])).astype(jnp.bfloat16)
    return (after.astype(jnp.float32) + dot(hidden, down_ref[...])).astype(jnp.bfloat16)


def inner_kernel(own_ref, qkv_ref, proj_ref, up_ref, down_ref, out_ref, query, key, value):
    step = pl.program_id(0)
    half = PATCH // 2
    steps = out_ref.shape[0] // half

    @pl.when(step == 0)
    def _():
        for part in range(steps):
            at = part * half
            project(own_ref[at + half : at + 2 * half, :], at, at, qkv_ref, key, value, query, at)

    first = pl.multiple_of(step * half, half)
    start = pl.multiple_of(PATCH * (step // 2), PATCH)
    residual = own_ref[pl.ds(first + half, half), :]
    out_ref[pl.ds(first, half), :] = transform(residual, first, start, query, key, value, proj_ref, up_ref, down_ref)


def outer_kernel(
    index_ref,
    left_ref,
    own_ref,
    right_ref,
    inner_ref,
    qkv_ref,
    proj_ref,
    up_ref,
    down_ref,
    send_ref,
    query,
    key,
    value,
    pairs,
    table,
):
    step = pl.program_id(0)
    rows = own_ref.shape[0]
    half = PATCH // 2

    def deliver(values, row):
        for side in range(2):
            pairs[pl.ds(side, half, stride=2), :] = values[:, side * LANES : (side + 1) * LANES].astype(jnp.float32)

        def body(part, carry):
            base = pl.multiple_of(part * LANES, LANES)
            for other in range(LANES):
                slot = pl.multiple_of(index_ref[0, row + base + other], 2)
                table[pl.ds(slot, 2), :] = pairs[pl.ds(2 * base + 2 * other, 2), :]
            return carry

        lax.fori_loop(0, half // LANES, body, 0)

    @pl.when(step == 0)
    def _():
        project(left_ref[...], 0, 0, qkv_ref, key, value)
        project(own_ref[:half, :], half, half, qkv_ref, key, value, query, 0)
        project(own_ref[rows - half :, :], 2 * half, 2 * half, qkv_ref, key, value, query, half)
        project(right_ref[...], 3 * half, 3 * half, qkv_ref, key, value)

        def body(part, carry):
            at = pl.multiple_of(part * half, half)
            deliver(inner_ref[pl.ds(at, half), :], at + half)
            return carry

        lax.fori_loop(0, inner_ref.shape[0] // half, body, 0)

    row = pl.multiple_of(step * (rows - half), half)
    first = pl.multiple_of(step * half, half)
    start = pl.multiple_of(step * PATCH, PATCH)
    residual = own_ref[pl.ds(row, half), :]
    deliver(transform(residual, first, start, query, key, value, proj_ref, up_ref, down_ref), row)

    @pl.when(step == pl.num_programs(0) - 1)
    def _():
        slots = send_ref.shape[0]
        for side in range(2):
            send_ref[:, side * LANES : (side + 1) * LANES] = table[pl.ds(side, slots, stride=2), :].astype(jnp.bfloat16)


def inner_block(own, qkv, proj, up, down):
    rows, channels = own.shape
    half = PATCH // 2
    count = rows - 2 * half
    vmem = pl.BlockSpec(memory_space=pltpu.VMEM)
    return pl.pallas_call(
        inner_kernel,
        out_shape=jax.ShapeDtypeStruct((count, channels), jnp.bfloat16),
        grid=(count // half,),
        in_specs=[vmem] * 5,
        out_specs=vmem,
        scratch_shapes=[
            pltpu.VMEM((count, channels), jnp.bfloat16),
            pltpu.VMEM((channels, count), jnp.bfloat16),
            pltpu.VMEM((count, channels), jnp.bfloat16),
        ],
        compiler_params=pltpu.CompilerParams(vmem_limit_bytes=56 << 20),
        name="inner_block",
    )(own, qkv, proj, up, down)


def outer_block(index, left, own, right, inner, qkv, proj, up, down, slots):
    channels = own.shape[1]
    half = PATCH // 2
    vmem = pl.BlockSpec(memory_space=pltpu.VMEM)
    return pl.pallas_call(
        outer_kernel,
        out_shape=jax.ShapeDtypeStruct((slots, channels), jnp.bfloat16),
        grid=(2,),
        in_specs=[pl.BlockSpec(memory_space=pltpu.SMEM)] + [vmem] * 8,
        out_specs=vmem,
        scratch_shapes=[
            pltpu.VMEM((2 * half, channels), jnp.bfloat16),
            pltpu.VMEM((channels, 2 * PATCH), jnp.bfloat16),
            pltpu.VMEM((2 * PATCH, channels), jnp.bfloat16),
            pltpu.VMEM((2 * half, LANES), jnp.float32),
            pltpu.VMEM((2 * slots, LANES), jnp.float32),
        ],
        compiler_params=pltpu.CompilerParams(vmem_limit_bytes=56 << 20),
        name="outer_block",
    )(index, left, own, right, inner, qkv, proj, up, down)


def settle_kernel(spans, place_ref, got_ref, *refs):
    outs, (pairs, table) = refs[: len(spans)], refs[len(spans) :]
    slots = got_ref.shape[0]
    capacity = place_ref.shape[1]
    for side in range(2):
        pairs[pl.ds(side, slots, stride=2), :] = got_ref[:, side * LANES : (side + 1) * LANES].astype(jnp.float32)

    def body(source, carry):
        base = pl.multiple_of(source * (2 * capacity), 2 * capacity)
        for slot in range(capacity):
            target = pl.multiple_of(place_ref[source, slot] + 6, 2)
            table[pl.ds(target, 2), :] = pairs[pl.ds(base + 2 * slot, 2), :]
        return carry

    lax.fori_loop(0, place_ref.shape[0], body, 0)
    for (first, count), out_ref in zip(spans, outs):
        for side in range(2):
            out_ref[:, side * LANES : (side + 1) * LANES] = table[
                pl.ds(8 + 2 * first + side, count, stride=2), :
            ].astype(jnp.bfloat16)


def settle(place, got, rows, spans):
    slots, channels = got.shape
    vmem = pl.BlockSpec(memory_space=pltpu.VMEM)
    return pl.pallas_call(
        functools.partial(settle_kernel, spans),
        out_shape=tuple(jax.ShapeDtypeStruct((count, channels), jnp.bfloat16) for _, count in spans),
        in_specs=[pl.BlockSpec(memory_space=pltpu.SMEM), vmem],
        out_specs=(vmem,) * len(spans),
        scratch_shapes=[pltpu.VMEM((2 * slots, LANES), jnp.float32), pltpu.VMEM((2 * rows + 8, LANES), jnp.float32)],
        compiler_params=pltpu.CompilerParams(vmem_limit_bytes=56 << 20),
        name="settle",
    )(place, got)


CHUNK = 32


def pick(step, values):
    return sum(jnp.where(step == place, value, 0) for place, value in enumerate(values) if value)


def conv_kernel(segment, starts, stores, sources, kept, rows, index_ref, *refs):
    parts, refs = refs[: len(sources)], refs[len(sources) :]
    olds, refs = refs[: len(kept)], refs[len(kept) :]
    weight_ref, linear_ref, out_ref, table, ping, pong, operand = refs
    step = pl.program_id(0)
    width = out_ref.shape[1]
    offsets = weight_ref.shape[0] // width
    middle = offsets // 2
    moved = offsets - 3
    block = 2 * segment
    sides = width // LANES

    @pl.when(step == 0)
    def _():
        for (first, count), ref in zip(sources, parts):
            for side in range(sides):
                table[pl.ds(2 * first + side, count, stride=2), :] = ref[:, side * LANES : (side + 1) * LANES].astype(
                    jnp.float32
                )
        table[pl.ds(6 * rows, 8), :] = jnp.zeros((8, LANES), jnp.float32)
        for first, ref in zip(kept, olds):
            out_ref[first : first + ref.shape[0], :] = ref[...]

    begins = [pl.multiple_of(pick(step, [pair[piece] for pair in starts]), segment) for piece in range(2)]
    ends = [pl.multiple_of(pick(step, [pair[piece] for pair in stores]), segment) for piece in range(2)]
    for span, offset in enumerate((0, middle, offsets - 1)):
        for piece, begin in enumerate(begins):
            for side in range(sides):
                operand[
                    piece * segment : (piece + 1) * segment,
                    offset * width + side * LANES : offset * width + (side + 1) * LANES,
                ] = table[pl.ds(2 * (span * rows + begin) + side, segment, stride=2), :].astype(jnp.bfloat16)

    def fetch(order, buffer, row):
        for other in range(row, row + CHUNK):
            source = pl.multiple_of(index_ref[0, 0, order * block + other], 2)
            buffer[2 * other : 2 * other + 2, :] = table[pl.ds(source, 2), :]

    def settle_columns(order, buffer, row):
        offset = order + jnp.where(order < middle - 1, 1, 2)
        column = pl.multiple_of(offset * width, width)
        halves = [buffer[pl.ds(2 * row + side, CHUNK, stride=2), :].astype(jnp.bfloat16) for side in range(sides)]
        operand[row : row + CHUNK, pl.ds(column, width)] = jnp.concatenate(halves, axis=1)

    def body(pair, carry):
        for turn, (filled, other) in enumerate(((ping, pong), (pong, ping))):
            order = 2 * pair + turn
            for row in range(0, block, CHUNK):
                fetch(order, filled, row)
                settle_columns(jnp.maximum(order - 1, 0), other, row)
        return carry

    lax.fori_loop(0, moved // 2, body, 0)
    for row in range(0, block, CHUNK):
        settle_columns(jnp.int32(moved - 1), pong, row)
    conv = dot(operand[...], weight_ref[...]).astype(jnp.bfloat16)
    normed = layer_norm(dot(conv, linear_ref[...]))
    for piece in range(2):
        begin = 2 * (rows + begins[piece])
        own = [table[pl.ds(begin + side, segment, stride=2), :] for side in range(sides)]
        result = jnp.concatenate(own, axis=1) + normed[piece * segment : (piece + 1) * segment]
        out_ref[pl.ds(ends[piece], segment), :] = result.astype(jnp.bfloat16)


def position_conv(near, starts, stores, count, sources, parts, kept, olds, weight, linear):
    rows, offsets = near.shape
    channels = linear.shape[0]
    segment = rows // 8
    middle = offsets // 2
    steps = len(starts)
    row_id = jnp.arange(rows, dtype=jnp.int32)[:, None]
    index = 2 * jnp.where(near < 0, 3 * rows, near + row_id)
    index = jnp.concatenate([index[:, 1:middle], index[:, middle + 1 : offsets - 1]], axis=1)
    index = jnp.concatenate([index[begin : begin + segment] for pair in starts for begin in pair], axis=0)
    index = index.reshape(steps, 2 * segment, offsets - 3).transpose(0, 2, 1).reshape(steps, 1, -1)
    vmem = pl.BlockSpec(memory_space=pltpu.VMEM)
    return pl.pallas_call(
        functools.partial(conv_kernel, segment, starts, stores, sources, kept, rows),
        out_shape=jax.ShapeDtypeStruct((count, channels), jnp.bfloat16),
        grid=(steps,),
        in_specs=[pl.BlockSpec((1, 1, index.shape[2]), lambda step: (step, 0, 0), memory_space=pltpu.SMEM)]
        + [vmem] * (len(parts) + len(olds) + 2),
        out_specs=vmem,
        scratch_shapes=[
            pltpu.VMEM((6 * rows + 8, LANES), jnp.float32),
            pltpu.VMEM((4 * segment, LANES), jnp.float32),
            pltpu.VMEM((4 * segment, LANES), jnp.float32),
            pltpu.VMEM((2 * segment, offsets * channels), jnp.bfloat16),
        ],
        compiler_params=pltpu.CompilerParams(vmem_limit_bytes=56 << 20),
        name="position_conv",
    )(index, *parts, *olds, weight, linear)


def on_device(
    points,
    qkv_one,
    proj_one,
    up_one,
    down_one,
    hilbert_device,
    hilbert_position,
    neighbors,
    conv_two,
    linear_two,
):
    row_count, channels = points.shape
    half = PATCH // 2
    devices = lax.axis_size(AXES)
    capacity = 2 * row_count // devices
    ring_up = [(i, (i + 1) % devices) for i in range(devices)]
    ring_down = [((i + 1) % devices, i) for i in range(devices)]
    before = lax.ppermute(points[row_count - half :], AXES, ring_up)
    behind = lax.ppermute(points[:half], AXES, ring_down)
    inner = inner_block(points, qkv_one, proj_one, up_one, down_one)
    inner, hilbert_device = lax.optimization_barrier((inner, hilbert_device))
    index, place = find_slots(hilbert_device, hilbert_position, devices, capacity)
    got_place = lax.all_to_all(place, AXES, split_axis=0, concat_axis=0, tiled=True)
    send = outer_block(
        index, before, points, behind, inner, qkv_one, proj_one, up_one, down_one, devices * capacity
    )
    got = lax.all_to_all(
        send.reshape(devices, capacity, channels), AXES, split_axis=0, concat_axis=0, tiled=True
    )
    segment = row_count // 8
    low, high = 3 * segment, 5 * segment
    spans = ((0, row_count), (low, row_count - low), (0, high), (0, low), (high, row_count - high))
    serial, upper_near, lower_near, lower_far, upper_far = settle(
        got_place, got.reshape(devices * capacity, channels), row_count, spans
    )
    left_near = lax.ppermute(upper_near, AXES, ring_up[:-1])
    right_near = lax.ppermute(lower_near, AXES, ring_down[:-1])
    left_far = lax.ppermute(lower_far, AXES, ring_up[:-1])
    right_far = lax.ppermute(upper_far, AXES, ring_down[:-1])
    parts = [left_near, serial, right_near]
    sources = [(low, row_count - low), (row_count, row_count), (2 * row_count, high)]
    inner = [(low, low + segment)]
    outer = [(0, segment), (2 * segment, high), (6 * segment, 7 * segment)]
    center = position_conv(
        neighbors, inner, [(0, segment)], 2 * segment, sources, parts, [], [], conv_two, linear_two
    )
    parts += [left_far, right_far]
    sources += [(0, low), (2 * row_count + high, row_count - high)]
    return position_conv(
        neighbors, outer, outer, row_count, sources, parts, [low], [center], conv_two, linear_two
    )


def solution(mesh):
    split = P(AXES)
    rows = P(AXES, None)
    return jax.shard_map(
        on_device,
        mesh=mesh,
        in_specs=(rows, P(), P(), P(), P(), split, split, rows, P(), P()),
        out_specs=rows,
        check_vma=False,
    )
```

```python
import functools

import jax
import jax.numpy as jnp
from jax import lax
from jax.experimental import pallas as pl
from jax.experimental.pallas import tpu as pltpu
from jax.sharding import PartitionSpec as P

HEADS = 16
HEAD_DIM = 16
PATCH = 1024
LANES = 128
EPS = 1e-05
LOG2E = 1.4426950408889634
AXES = ("curve", "group")


def layer_norm(values):
    values = values.astype(jnp.float32)
    center = jnp.mean(values, axis=-1, keepdims=True)
    offset = values - center
    spread = jnp.mean(offset * offset, axis=-1, keepdims=True)
    return offset * lax.rsqrt(spread + EPS)


def dot(left, right):
    return jnp.dot(left, right, preferred_element_type=jnp.float32)


def gelu(values):
    return 0.5 * values * (1.0 + lax.erf(values * 0.7071067811865476))


def slots_kernel(devices, capacity, device_ref, position_ref, index_ref, place_ref):
    rows = device_ref.shape[1]
    chunk = min(256, rows)
    row_id = lax.broadcasted_iota(jnp.int32, (chunk, chunk), 0)
    col_id = lax.broadcasted_iota(jnp.int32, (chunk, chunk), 1)
    before = (row_id <= col_id).astype(jnp.float32).astype(jnp.bfloat16)
    device_id = lax.broadcasted_iota(jnp.int32, (devices, chunk), 0)
    slot_id = lax.broadcasted_iota(jnp.int32, (capacity, chunk), 0)
    carry = jnp.zeros((devices, 1), jnp.float32)
    place = jnp.zeros((2 * devices, capacity), jnp.float32)
    for part in range(rows // chunk):
        span = slice(part * chunk, (part + 1) * chunk)
        target = device_ref[:, span]
        mine = (device_id == target).astype(jnp.float32)
        running = dot(mine.astype(jnp.bfloat16), before) + carry
        carry = running[:, chunk - 1 : chunk]
        slot = (jnp.sum(mine * running, axis=0, keepdims=True) - 1.0).astype(jnp.int32)
        index_ref[:, span] = 2 * (target * capacity + slot)
        code = position_ref[:, span] + 1
        high = mine * (code // LANES).astype(jnp.float32)
        low = mine * (code % LANES).astype(jnp.float32)
        here = (slot_id == slot).astype(jnp.float32).astype(jnp.bfloat16)
        place += lax.dot_general(
            jnp.concatenate([high, low], axis=0).astype(jnp.bfloat16),
            here,
            (((1,), (1,)), ((), ())),
            preferred_element_type=jnp.float32,
        )
    place_ref[...] = 2 * (place[:devices] * float(LANES) + place[devices:]).astype(jnp.int32)


def find_slots(device, position, devices, capacity):
    rows = device.shape[0]
    return pl.pallas_call(
        functools.partial(slots_kernel, devices, capacity),
        out_shape=(
            jax.ShapeDtypeStruct((1, rows), jnp.int32),
            jax.ShapeDtypeStruct((devices, capacity), jnp.int32),
        ),
        name="find_slots",
    )(device.reshape(1, rows), position.reshape(1, rows))


def project(source, key, value, weight_ref, key_ref, value_ref, query_ref=None, query=0):
    count, channels = source.shape
    normed = layer_norm(source).astype(jnp.bfloat16)
    key_ref[:, key : key + count] = lax.dot_general(
        weight_ref[:, channels : 2 * channels],
        normed,
        (((0,), (1,)), ((), ())),
        preferred_element_type=jnp.float32,
    ).astype(jnp.bfloat16)
    value_ref[value : value + count, :] = dot(normed, weight_ref[:, 2 * channels :]).astype(jnp.bfloat16)
    if query_ref is not None:
        query_ref[query : query + count, :] = dot(normed, weight_ref[:, :channels]).astype(jnp.bfloat16)


def transform(residual, first, start, query, key, value, proj_ref, up_ref, down_ref):
    half, channels = residual.shape
    per_group = LANES // HEAD_DIM
    head_of = lax.broadcasted_iota(jnp.int32, (1, LANES), 1) // HEAD_DIM
    scale = HEAD_DIM ** (-0.5) * LOG2E
    pieces = []
    for group in range(channels // LANES):
        lanes = slice(group * LANES, (group + 1) * LANES)
        queries = query[pl.ds(first, half), lanes]
        keys = key[lanes, pl.ds(start, PATCH)]
        values = value[pl.ds(start, PATCH), lanes]
        total = None
        for head in range(per_group):
            mine = head_of == head
            scores = dot(jnp.where(mine, queries, jnp.zeros_like(queries)), keys)
            peak = jnp.max(scores, axis=1, keepdims=True)
            weights = jnp.exp2((scores - peak) * scale).astype(jnp.bfloat16)
            ones = jnp.broadcast_to(mine.astype(jnp.float32).astype(jnp.bfloat16), values.shape)
            both = jnp.concatenate([jnp.where(mine, values, jnp.zeros_like(values)), ones], axis=1)
            result = dot(weights, both)
            total = result if total is None else total + result
        pieces.append((total[:, :LANES] / total[:, LANES:]).astype(jnp.bfloat16))
    mixed = jnp.concatenate(pieces, axis=1)
    after = (residual.astype(jnp.float32) + dot(mixed, proj_ref[...])).astype(jnp.bfloat16)
    normed = layer_norm(after).astype(jnp.bfloat16)
    hidden = gelu(dot(normed, up_ref[...])).astype(jnp.bfloat16)
    return (after.astype(jnp.float32) + dot(hidden, down_ref[...])).astype(jnp.bfloat16)


def inner_kernel(own_ref, qkv_ref, proj_ref, up_ref, down_ref, out_ref, query, key, value):
    step = pl.program_id(0)
    half = PATCH // 2
    steps = out_ref.shape[0] // half

    @pl.when(step == 0)
    def _():
        for part in range(steps):
            at = part * half
            project(own_ref[at + half : at + 2 * half, :], at, at, qkv_ref, key, value, query, at)

    first = pl.multiple_of(step * half, half)
    start = pl.multiple_of(PATCH * (step // 2), PATCH)
    residual = own_ref[pl.ds(first + half, half), :]
    out_ref[pl.ds(first, half), :] = transform(residual, first, start, query, key, value, proj_ref, up_ref, down_ref)


def outer_kernel(
    index_ref,
    left_ref,
    own_ref,
    right_ref,
    inner_ref,
    qkv_ref,
    proj_ref,
    up_ref,
    down_ref,
    send_ref,
    query,
    key,
    value,
    pairs,
    table,
):
    step = pl.program_id(0)
    rows = own_ref.shape[0]
    half = PATCH // 2

    def deliver(values, row):
        for side in range(2):
            pairs[pl.ds(side, half, stride=2), :] = values[:, side * LANES : (side + 1) * LANES].astype(jnp.float32)

        def body(part, carry):
            base = pl.multiple_of(part * LANES, LANES)
            for other in range(LANES):
                slot = pl.multiple_of(index_ref[0, row + base + other], 2)
                table[pl.ds(slot, 2), :] = pairs[pl.ds(2 * base + 2 * other, 2), :]
            return carry

        lax.fori_loop(0, half // LANES, body, 0)

    @pl.when(step == 0)
    def _():
        project(left_ref[...], 0, 0, qkv_ref, key, value)
        project(own_ref[:half, :], half, half, qkv_ref, key, value, query, 0)
        project(own_ref[rows - half :, :], 2 * half, 2 * half, qkv_ref, key, value, query, half)
        project(right_ref[...], 3 * half, 3 * half, qkv_ref, key, value)

        def body(part, carry):
            at = pl.multiple_of(part * half, half)
            deliver(inner_ref[pl.ds(at, half), :], at + half)
            return carry

        lax.fori_loop(0, inner_ref.shape[0] // half, body, 0)

    row = pl.multiple_of(step * (rows - half), half)
    first = pl.multiple_of(step * half, half)
    start = pl.multiple_of(step * PATCH, PATCH)
    residual = own_ref[pl.ds(row, half), :]
    deliver(transform(residual, first, start, query, key, value, proj_ref, up_ref, down_ref), row)

    @pl.when(step == pl.num_programs(0) - 1)
    def _():
        slots = send_ref.shape[0]
        for side in range(2):
            send_ref[:, side * LANES : (side + 1) * LANES] = table[pl.ds(side, slots, stride=2), :].astype(jnp.bfloat16)


def inner_block(own, qkv, proj, up, down):
    rows, channels = own.shape
    half = PATCH // 2
    count = rows - 2 * half
    vmem = pl.BlockSpec(memory_space=pltpu.VMEM)
    return pl.pallas_call(
        inner_kernel,
        out_shape=jax.ShapeDtypeStruct((count, channels), jnp.bfloat16),
        grid=(count // half,),
        in_specs=[vmem] * 5,
        out_specs=vmem,
        scratch_shapes=[
            pltpu.VMEM((count, channels), jnp.bfloat16),
            pltpu.VMEM((channels, count), jnp.bfloat16),
            pltpu.VMEM((count, channels), jnp.bfloat16),
        ],
        compiler_params=pltpu.CompilerParams(vmem_limit_bytes=56 << 20),
        name="inner_block",
    )(own, qkv, proj, up, down)


def outer_block(index, left, own, right, inner, qkv, proj, up, down, slots):
    channels = own.shape[1]
    half = PATCH // 2
    vmem = pl.BlockSpec(memory_space=pltpu.VMEM)
    return pl.pallas_call(
        outer_kernel,
        out_shape=jax.ShapeDtypeStruct((slots, channels), jnp.bfloat16),
        grid=(2,),
        in_specs=[pl.BlockSpec(memory_space=pltpu.SMEM)] + [vmem] * 8,
        out_specs=vmem,
        scratch_shapes=[
            pltpu.VMEM((2 * half, channels), jnp.bfloat16),
            pltpu.VMEM((channels, 2 * PATCH), jnp.bfloat16),
            pltpu.VMEM((2 * PATCH, channels), jnp.bfloat16),
            pltpu.VMEM((2 * half, LANES), jnp.float32),
            pltpu.VMEM((2 * slots, LANES), jnp.float32),
        ],
        compiler_params=pltpu.CompilerParams(vmem_limit_bytes=56 << 20),
        name="outer_block",
    )(index, left, own, right, inner, qkv, proj, up, down)


def settle_kernel(spans, place_ref, got_ref, *refs):
    outs, (pairs, table) = refs[: len(spans)], refs[len(spans) :]
    slots = got_ref.shape[0]
    capacity = place_ref.shape[1]
    for side in range(2):
        pairs[pl.ds(side, slots, stride=2), :] = got_ref[:, side * LANES : (side + 1) * LANES].astype(jnp.float32)

    def body(source, carry):
        base = pl.multiple_of(source * (2 * capacity), 2 * capacity)
        for slot in range(capacity):
            target = pl.multiple_of(place_ref[source, slot] + 6, 2)
            table[pl.ds(target, 2), :] = pairs[pl.ds(base + 2 * slot, 2), :]
        return carry

    lax.fori_loop(0, place_ref.shape[0], body, 0)
    for (first, count), out_ref in zip(spans, outs):
        for side in range(2):
            out_ref[:, side * LANES : (side + 1) * LANES] = table[
                pl.ds(8 + 2 * first + side, count, stride=2), :
            ].astype(jnp.bfloat16)


def settle(place, got, rows, spans):
    slots, channels = got.shape
    vmem = pl.BlockSpec(memory_space=pltpu.VMEM)
    return pl.pallas_call(
        functools.partial(settle_kernel, spans),
        out_shape=tuple(jax.ShapeDtypeStruct((count, channels), jnp.bfloat16) for _, count in spans),
        in_specs=[pl.BlockSpec(memory_space=pltpu.SMEM), vmem],
        out_specs=(vmem,) * len(spans),
        scratch_shapes=[pltpu.VMEM((2 * slots, LANES), jnp.float32), pltpu.VMEM((2 * rows + 8, LANES), jnp.float32)],
        compiler_params=pltpu.CompilerParams(vmem_limit_bytes=56 << 20),
        name="settle",
    )(place, got)


CHUNK = 32


def pick(step, values):
    return sum(jnp.where(step == place, value, 0) for place, value in enumerate(values) if value)


def conv_kernel(segment, starts, stores, sources, kept, rows, index_ref, *refs):
    parts, refs = refs[: len(sources)], refs[len(sources) :]
    olds, refs = refs[: len(kept)], refs[len(kept) :]
    weight_ref, linear_ref, out_ref, table, ping, pong, summed = refs
    step = pl.program_id(0)
    width = out_ref.shape[1]
    offsets = weight_ref.shape[0] // width
    middle = offsets // 2
    moved = offsets - 3
    block = 2 * segment
    sides = width // LANES
    units = 2

    @pl.when(step == 0)
    def _():
        for (first, count), ref in zip(sources, parts):
            for side in range(sides):
                table[pl.ds(2 * first + side, count, stride=2), :] = ref[:, side * LANES : (side + 1) * LANES].astype(
                    jnp.float32
                )
        table[pl.ds(6 * rows, 8), :] = jnp.zeros((8, LANES), jnp.float32)
        for first, ref in zip(kept, olds):
            out_ref[first : first + ref.shape[0], :] = ref[...]

    begins = [pl.multiple_of(pick(step, [pair[piece] for pair in starts]), segment) for piece in range(2)]
    ends = [pl.multiple_of(pick(step, [pair[piece] for pair in stores]), segment) for piece in range(2)]

    def fetch(order, buffer, row):
        for other in range(row, row + CHUNK):
            source = pl.multiple_of(index_ref[0, 0, order * block + other], 2)
            buffer[2 * other : 2 * other + 2, :] = table[pl.ds(source, 2), :]

    def moved_rows(buffer, row):
        return [buffer[pl.ds(2 * row + side, CHUNK, stride=2), :] for side in range(sides)]

    def span_rows(span, row):
        begin = 2 * (span * rows + begins[row // segment] + row % segment)
        return [table[pl.ds(begin + side, CHUNK, stride=2), :] for side in range(sides)]

    def column(order):
        return order + jnp.where(order < middle - 1, 1, 2)

    def accumulate(*sums):
        def stage(offset, staging, take, order=None, buffer=None):
            weight = weight_ref[pl.ds(pl.multiple_of(offset * width, width), width), :]
            for unit in range(units):
                pltpu.matmul_push_rhs(weight, staging, unit)
            for place, row in enumerate(range(0, block, CHUNK)):
                if buffer is not None:
                    fetch(order, buffer, row)
                left = jnp.concatenate([half.astype(jnp.bfloat16) for half in take(row)], axis=1)
                pltpu.matmul_acc_lhs(sums[place], left, load_staged_rhs=staging if place < units else None)

        for place, row in enumerate(range(0, block, CHUNK)):
            summed[row : row + CHUNK, :] = pltpu.matmul_pop(sums[place])
        stage(0, 0, functools.partial(span_rows, 0), 0, ping)
        stage(middle, 1, functools.partial(span_rows, 1))
        stage(offsets - 1, 0, functools.partial(span_rows, 2))

        def body(pair, carry):
            order = 2 * pair
            stage(column(order), 1, functools.partial(moved_rows, ping), order + 1, pong)
            stage(column(order + 1), 0, functools.partial(moved_rows, pong), order + 2, ping)
            return carry

        lax.fori_loop(0, moved // 2 - 1, body, 0)
        stage(column(jnp.int32(moved - 2)), 1, functools.partial(moved_rows, ping), moved - 1, pong)
        stage(column(jnp.int32(moved - 1)), 0, functools.partial(moved_rows, pong))
        for place, row in enumerate(range(0, block, CHUNK)):
            if place < units:
                pltpu.matmul_push_rhs(linear_ref[...], 1, place)
            conv = pltpu.matmul_pop(sums[place]).astype(jnp.bfloat16)
            pltpu.matmul_acc_lhs(sums[place], conv, load_staged_rhs=1 if place < units else None)
        for place, row in enumerate(range(0, block, CHUNK)):
            summed[row : row + CHUNK, :] = pltpu.matmul_pop(sums[place])

    chunks = range(block // CHUNK)
    pl.run_scoped(accumulate, *[pltpu.ACC(place % units)((CHUNK, width), jnp.float32) for place in chunks])
    normed = layer_norm(summed[...])
    for piece in range(2):
        begin = 2 * (rows + begins[piece])
        own = [table[pl.ds(begin + side, segment, stride=2), :] for side in range(sides)]
        result = jnp.concatenate(own, axis=1) + normed[piece * segment : (piece + 1) * segment]
        out_ref[pl.ds(ends[piece], segment), :] = result.astype(jnp.bfloat16)


def position_conv(near, starts, stores, count, sources, parts, kept, olds, weight, linear):
    rows, offsets = near.shape
    channels = linear.shape[0]
    segment = rows // 8
    middle = offsets // 2
    steps = len(starts)
    row_id = jnp.arange(rows, dtype=jnp.int32)[:, None]
    index = 2 * jnp.where(near < 0, 3 * rows, near + row_id)
    index = jnp.concatenate([index[:, 1:middle], index[:, middle + 1 : offsets - 1]], axis=1)
    index = jnp.concatenate([index[begin : begin + segment] for pair in starts for begin in pair], axis=0)
    index = index.reshape(steps, 2 * segment, offsets - 3).transpose(0, 2, 1).reshape(steps, 1, -1)
    vmem = pl.BlockSpec(memory_space=pltpu.VMEM)
    return pl.pallas_call(
        functools.partial(conv_kernel, segment, starts, stores, sources, kept, rows),
        out_shape=jax.ShapeDtypeStruct((count, channels), jnp.bfloat16),
        grid=(steps,),
        in_specs=[pl.BlockSpec((1, 1, index.shape[2]), lambda step: (step, 0, 0), memory_space=pltpu.SMEM)]
        + [vmem] * (len(parts) + len(olds) + 2),
        out_specs=vmem,
        scratch_shapes=[
            pltpu.VMEM((6 * rows + 8, LANES), jnp.float32),
            pltpu.VMEM((4 * segment, LANES), jnp.float32),
            pltpu.VMEM((4 * segment, LANES), jnp.float32),
            pltpu.VMEM((2 * segment, channels), jnp.float32),
        ],
        compiler_params=pltpu.CompilerParams(vmem_limit_bytes=20 << 20),
        name="position_conv",
    )(index, *parts, *olds, weight, linear)


def on_device(
    points,
    qkv_one,
    proj_one,
    up_one,
    down_one,
    hilbert_device,
    hilbert_position,
    neighbors,
    conv_two,
    linear_two,
):
    row_count, channels = points.shape
    half = PATCH // 2
    devices = lax.axis_size(AXES)
    capacity = 2 * row_count // devices
    ring_up = [(i, (i + 1) % devices) for i in range(devices)]
    ring_down = [((i + 1) % devices, i) for i in range(devices)]
    before = lax.ppermute(points[row_count - half :], AXES, ring_up)
    behind = lax.ppermute(points[:half], AXES, ring_down)
    inner = inner_block(points, qkv_one, proj_one, up_one, down_one)
    inner, hilbert_device = lax.optimization_barrier((inner, hilbert_device))
    index, place = find_slots(hilbert_device, hilbert_position, devices, capacity)
    got_place = lax.all_to_all(place, AXES, split_axis=0, concat_axis=0, tiled=True)
    send = outer_block(
        index, before, points, behind, inner, qkv_one, proj_one, up_one, down_one, devices * capacity
    )
    got = lax.all_to_all(
        send.reshape(devices, capacity, channels), AXES, split_axis=0, concat_axis=0, tiled=True
    )
    segment = row_count // 8
    low, high = 3 * segment, 5 * segment
    spans = ((0, row_count), (low, row_count - low), (0, high), (0, low), (high, row_count - high))
    serial, upper_near, lower_near, lower_far, upper_far = settle(
        got_place, got.reshape(devices * capacity, channels), row_count, spans
    )
    left_near = lax.ppermute(upper_near, AXES, ring_up[:-1])
    right_near = lax.ppermute(lower_near, AXES, ring_down[:-1])
    left_far = lax.ppermute(lower_far, AXES, ring_up[:-1])
    right_far = lax.ppermute(upper_far, AXES, ring_down[:-1])
    parts = [left_near, serial, right_near]
    sources = [(low, row_count - low), (row_count, row_count), (2 * row_count, high)]
    inner = [(low, low + segment)]
    outer = [(0, segment), (2 * segment, high), (6 * segment, 7 * segment)]
    center = position_conv(
        neighbors, inner, [(0, segment)], 2 * segment, sources, parts, [], [], conv_two, linear_two
    )
    parts += [left_far, right_far]
    sources += [(0, low), (2 * row_count + high, row_count - high)]
    return position_conv(
        neighbors, outer, outer, row_count, sources, parts, [low], [center], conv_two, linear_two
    )


def solution(mesh):
    split = P(AXES)
    rows = P(AXES, None)
    return jax.shard_map(
        on_device,
        mesh=mesh,
        in_specs=(rows, P(), P(), P(), P(), split, split, rows, P(), P()),
        out_specs=rows,
        check_vma=False,
    )
```

```python
import functools

import jax
import jax.numpy as jnp
from jax import lax
from jax.experimental import pallas as pl
from jax.experimental.pallas import tpu as pltpu
from jax.sharding import PartitionSpec as P

HEADS = 16
HEAD_DIM = 16
PATCH = 1024
LANES = 128
EPS = 1e-05
LOG2E = 1.4426950408889634
AXES = ("curve", "group")


def layer_norm(values):
    values = values.astype(jnp.float32)
    center = jnp.mean(values, axis=-1, keepdims=True)
    offset = values - center
    spread = jnp.mean(offset * offset, axis=-1, keepdims=True)
    return offset * lax.rsqrt(spread + EPS)


def dot(left, right):
    return jnp.dot(left, right, preferred_element_type=jnp.float32)


def gelu(values):
    return 0.5 * values * (1.0 + lax.erf(values * 0.7071067811865476))


def slots_kernel(devices, capacity, device_ref, position_ref, index_ref, place_ref):
    rows = device_ref.shape[1]
    chunk = min(256, rows)
    row_id = lax.broadcasted_iota(jnp.int32, (chunk, chunk), 0)
    col_id = lax.broadcasted_iota(jnp.int32, (chunk, chunk), 1)
    before = (row_id <= col_id).astype(jnp.float32).astype(jnp.bfloat16)
    device_id = lax.broadcasted_iota(jnp.int32, (devices, chunk), 0)
    slot_id = lax.broadcasted_iota(jnp.int32, (capacity, chunk), 0)
    carry = jnp.zeros((devices, 1), jnp.float32)
    place = jnp.zeros((2 * devices, capacity), jnp.float32)
    for part in range(rows // chunk):
        span = slice(part * chunk, (part + 1) * chunk)
        target = device_ref[:, span]
        mine = (device_id == target).astype(jnp.float32)
        running = dot(mine.astype(jnp.bfloat16), before) + carry
        carry = running[:, chunk - 1 : chunk]
        slot = (jnp.sum(mine * running, axis=0, keepdims=True) - 1.0).astype(jnp.int32)
        index_ref[:, span] = 2 * (target * capacity + slot)
        code = position_ref[:, span] + 1
        high = mine * (code // LANES).astype(jnp.float32)
        low = mine * (code % LANES).astype(jnp.float32)
        here = (slot_id == slot).astype(jnp.float32).astype(jnp.bfloat16)
        place += lax.dot_general(
            jnp.concatenate([high, low], axis=0).astype(jnp.bfloat16),
            here,
            (((1,), (1,)), ((), ())),
            preferred_element_type=jnp.float32,
        )
    place_ref[...] = 2 * (place[:devices] * float(LANES) + place[devices:]).astype(jnp.int32)


def find_slots(device, position, devices, capacity):
    rows = device.shape[0]
    return pl.pallas_call(
        functools.partial(slots_kernel, devices, capacity),
        out_shape=(
            jax.ShapeDtypeStruct((1, rows), jnp.int32),
            jax.ShapeDtypeStruct((devices, capacity), jnp.int32),
        ),
        name="find_slots",
    )(device.reshape(1, rows), position.reshape(1, rows))


def project(source, key, value, weight_ref, key_ref, value_ref, query_ref=None, query=0):
    count, channels = source.shape
    normed = layer_norm(source).astype(jnp.bfloat16)
    key_ref[:, key : key + count] = lax.dot_general(
        weight_ref[:, channels : 2 * channels],
        normed,
        (((0,), (1,)), ((), ())),
        preferred_element_type=jnp.float32,
    ).astype(jnp.bfloat16)
    value_ref[value : value + count, :] = dot(normed, weight_ref[:, 2 * channels :]).astype(jnp.bfloat16)
    if query_ref is not None:
        query_ref[query : query + count, :] = dot(normed, weight_ref[:, :channels]).astype(jnp.bfloat16)


def transform(residual, first, start, query, key, value, proj_ref, up_ref, down_ref):
    half, channels = residual.shape
    per_group = LANES // HEAD_DIM
    head_of = lax.broadcasted_iota(jnp.int32, (1, LANES), 1) // HEAD_DIM
    scale = HEAD_DIM ** (-0.5) * LOG2E
    pieces = []
    for group in range(channels // LANES):
        lanes = slice(group * LANES, (group + 1) * LANES)
        queries = query[pl.ds(first, half), lanes]
        keys = key[lanes, pl.ds(start, PATCH)]
        values = value[pl.ds(start, PATCH), lanes]
        total = None
        for head in range(0, per_group, 2):
            masks = [head_of == head + turn for turn in range(2)]
            stacked = jnp.concatenate([jnp.where(mine, queries, jnp.zeros_like(queries)) for mine in masks], axis=0)
            both_scores = dot(stacked, keys)
            for turn, mine in enumerate(masks):
                scores = both_scores[turn * half : (turn + 1) * half]
                peak = jnp.max(scores, axis=1, keepdims=True)
                weights = jnp.exp2((scores - peak) * scale).astype(jnp.bfloat16)
                ones = jnp.broadcast_to(mine.astype(jnp.float32).astype(jnp.bfloat16), values.shape)
                both = jnp.concatenate([jnp.where(mine, values, jnp.zeros_like(values)), ones], axis=1)
                result = dot(weights, both)
                total = result if total is None else total + result
        pieces.append((total[:, :LANES] / total[:, LANES:]).astype(jnp.bfloat16))
    mixed = jnp.concatenate(pieces, axis=1)
    after = (residual.astype(jnp.float32) + dot(mixed, proj_ref[...])).astype(jnp.bfloat16)
    normed = layer_norm(after).astype(jnp.bfloat16)
    hidden = gelu(dot(normed, up_ref[...])).astype(jnp.bfloat16)
    return (after.astype(jnp.float32) + dot(hidden, down_ref[...])).astype(jnp.bfloat16)


def inner_kernel(own_ref, qkv_ref, proj_ref, up_ref, down_ref, out_ref, query, key, value):
    step = pl.program_id(0)
    half = PATCH // 2
    steps = out_ref.shape[0] // half

    @pl.when(step == 0)
    def _():
        for part in range(steps):
            at = part * half
            project(own_ref[at + half : at + 2 * half, :], at, at, qkv_ref, key, value, query, at)

    first = pl.multiple_of(step * half, half)
    start = pl.multiple_of(PATCH * (step // 2), PATCH)
    residual = own_ref[pl.ds(first + half, half), :]
    out_ref[pl.ds(first, half), :] = transform(residual, first, start, query, key, value, proj_ref, up_ref, down_ref)


def outer_kernel(
    index_ref,
    left_ref,
    own_ref,
    right_ref,
    inner_ref,
    qkv_ref,
    proj_ref,
    up_ref,
    down_ref,
    send_ref,
    query,
    key,
    value,
    pairs,
    table,
):
    step = pl.program_id(0)
    rows = own_ref.shape[0]
    half = PATCH // 2

    def deliver(values, row):
        for side in range(2):
            pairs[pl.ds(side, half, stride=2), :] = values[:, side * LANES : (side + 1) * LANES].astype(jnp.float32)

        def body(part, carry):
            base = pl.multiple_of(part * LANES, LANES)
            for other in range(LANES):
                slot = pl.multiple_of(index_ref[0, row + base + other], 2)
                table[pl.ds(slot, 2), :] = pairs[pl.ds(2 * base + 2 * other, 2), :]
            return carry

        lax.fori_loop(0, half // LANES, body, 0)

    @pl.when(step == 0)
    def _():
        project(left_ref[...], 0, 0, qkv_ref, key, value)
        project(own_ref[:half, :], half, half, qkv_ref, key, value, query, 0)
        project(own_ref[rows - half :, :], 2 * half, 2 * half, qkv_ref, key, value, query, half)
        project(right_ref[...], 3 * half, 3 * half, qkv_ref, key, value)

        def body(part, carry):
            at = pl.multiple_of(part * half, half)
            deliver(inner_ref[pl.ds(at, half), :], at + half)
            return carry

        lax.fori_loop(0, inner_ref.shape[0] // half, body, 0)

    row = pl.multiple_of(step * (rows - half), half)
    first = pl.multiple_of(step * half, half)
    start = pl.multiple_of(step * PATCH, PATCH)
    residual = own_ref[pl.ds(row, half), :]
    deliver(transform(residual, first, start, query, key, value, proj_ref, up_ref, down_ref), row)

    @pl.when(step == pl.num_programs(0) - 1)
    def _():
        slots = send_ref.shape[0]
        for side in range(2):
            send_ref[:, side * LANES : (side + 1) * LANES] = table[pl.ds(side, slots, stride=2), :].astype(jnp.bfloat16)


def inner_block(own, qkv, proj, up, down):
    rows, channels = own.shape
    half = PATCH // 2
    count = rows - 2 * half
    vmem = pl.BlockSpec(memory_space=pltpu.VMEM)
    return pl.pallas_call(
        inner_kernel,
        out_shape=jax.ShapeDtypeStruct((count, channels), jnp.bfloat16),
        grid=(count // half,),
        in_specs=[vmem] * 5,
        out_specs=vmem,
        scratch_shapes=[
            pltpu.VMEM((count, channels), jnp.bfloat16),
            pltpu.VMEM((channels, count), jnp.bfloat16),
            pltpu.VMEM((count, channels), jnp.bfloat16),
        ],
        compiler_params=pltpu.CompilerParams(vmem_limit_bytes=56 << 20),
        name="inner_block",
    )(own, qkv, proj, up, down)


def outer_block(index, left, own, right, inner, qkv, proj, up, down, slots):
    channels = own.shape[1]
    half = PATCH // 2
    vmem = pl.BlockSpec(memory_space=pltpu.VMEM)
    return pl.pallas_call(
        outer_kernel,
        out_shape=jax.ShapeDtypeStruct((slots, channels), jnp.bfloat16),
        grid=(2,),
        in_specs=[pl.BlockSpec(memory_space=pltpu.SMEM)] + [vmem] * 8,
        out_specs=vmem,
        scratch_shapes=[
            pltpu.VMEM((2 * half, channels), jnp.bfloat16),
            pltpu.VMEM((channels, 2 * PATCH), jnp.bfloat16),
            pltpu.VMEM((2 * PATCH, channels), jnp.bfloat16),
            pltpu.VMEM((2 * half, LANES), jnp.float32),
            pltpu.VMEM((2 * slots, LANES), jnp.float32),
        ],
        compiler_params=pltpu.CompilerParams(vmem_limit_bytes=56 << 20),
        name="outer_block",
    )(index, left, own, right, inner, qkv, proj, up, down)


def settle_kernel(spans, place_ref, got_ref, *refs):
    outs, (pairs, table) = refs[: len(spans)], refs[len(spans) :]
    step = pl.program_id(0)
    slots = got_ref.shape[0]
    capacity = place_ref.shape[1]
    sources = slots // capacity
    for side in range(2):
        pairs[pl.ds(side, slots, stride=2), :] = got_ref[:, side * LANES : (side + 1) * LANES].astype(jnp.float32)

    def body(source, carry):
        base = pl.multiple_of(source * (2 * capacity), 2 * capacity)
        for slot in range(capacity):
            target = pl.multiple_of(place_ref[step * sources + source, slot] + 6, 2)
            table[pl.ds(target, 2), :] = pairs[pl.ds(base + 2 * slot, 2), :]
        return carry

    lax.fori_loop(0, sources, body, 0)

    @pl.when(step == pl.num_programs(0) - 1)
    def _():
        whole = outs[0]
        for side in range(2):
            whole[:, side * LANES : (side + 1) * LANES] = table[
                pl.ds(8 + side, whole.shape[0], stride=2), :
            ].astype(jnp.bfloat16)
        for (first, count), out_ref in zip(spans[1:], outs[1:]):
            out_ref[...] = whole[first : first + count, :]


def settle(place, got, rows, spans):
    slots, channels = got.shape
    steps = 8
    vmem = pl.BlockSpec(memory_space=pltpu.VMEM)
    return pl.pallas_call(
        functools.partial(settle_kernel, spans),
        out_shape=tuple(jax.ShapeDtypeStruct((count, channels), jnp.bfloat16) for _, count in spans),
        grid=(steps,),
        in_specs=[
            pl.BlockSpec(memory_space=pltpu.SMEM),
            pl.BlockSpec((slots // steps, channels), lambda step: (step, 0)),
        ],
        out_specs=(vmem,) * len(spans),
        scratch_shapes=[
            pltpu.VMEM((2 * slots // steps, LANES), jnp.float32),
            pltpu.VMEM((2 * rows + 8, LANES), jnp.float32),
        ],
        compiler_params=pltpu.CompilerParams(vmem_limit_bytes=56 << 20),
        name="settle",
    )(place, got)


CHUNK = 32


def pick(step, values):
    return sum(jnp.where(step == place, value, 0) for place, value in enumerate(values) if value)


def conv_kernel(segment, starts, stores, sources, kept, rows, index_ref, *refs):
    parts, refs = refs[: len(sources)], refs[len(sources) :]
    olds, refs = refs[: len(kept)], refs[len(kept) :]
    weight_ref, linear_ref, out_ref, table, ping, pong, summed = refs
    step = pl.program_id(0)
    width = out_ref.shape[1]
    offsets = weight_ref.shape[0] // width
    middle = offsets // 2
    moved = offsets - 3
    block = 2 * segment
    sides = width // LANES
    units = 2

    @pl.when(step == 0)
    def _():
        for (first, count), ref in zip(sources, parts):
            for side in range(sides):
                table[pl.ds(2 * first + side, count, stride=2), :] = ref[:, side * LANES : (side + 1) * LANES].astype(
                    jnp.float32
                )
        table[pl.ds(6 * rows, 8), :] = jnp.zeros((8, LANES), jnp.float32)
        for first, ref in zip(kept, olds):
            out_ref[first : first + ref.shape[0], :] = ref[...]

    begins = [pl.multiple_of(pick(step, [pair[piece] for pair in starts]), segment) for piece in range(2)]
    ends = [pl.multiple_of(pick(step, [pair[piece] for pair in stores]), segment) for piece in range(2)]

    def fetch(order, buffer, row):
        for other in range(row, row + CHUNK):
            source = pl.multiple_of(index_ref[0, 0, order * block + other], 2)
            buffer[2 * other : 2 * other + 2, :] = table[pl.ds(source, 2), :]

    def moved_rows(buffer, row):
        return [buffer[pl.ds(2 * row + side, CHUNK, stride=2), :] for side in range(sides)]

    def span_rows(span, row):
        begin = 2 * (span * rows + begins[row // segment] + row % segment)
        return [table[pl.ds(begin + side, CHUNK, stride=2), :] for side in range(sides)]

    def column(order):
        return order + jnp.where(order < middle - 1, 1, 2)

    def accumulate(*sums):
        def stage(offset, staging, take, order=None, buffer=None):
            weight = weight_ref[pl.ds(pl.multiple_of(offset * width, width), width), :]
            for unit in range(units):
                pltpu.matmul_push_rhs(weight, staging, unit)
            for place, row in enumerate(range(0, block, CHUNK)):
                if buffer is not None:
                    fetch(order, buffer, row)
                left = jnp.concatenate([half.astype(jnp.bfloat16) for half in take(row)], axis=1)
                pltpu.matmul_acc_lhs(sums[place], left, load_staged_rhs=staging if place < units else None)

        for place, row in enumerate(range(0, block, CHUNK)):
            summed[row : row + CHUNK, :] = pltpu.matmul_pop(sums[place])
        stage(0, 0, functools.partial(span_rows, 0), 0, ping)
        stage(middle, 1, functools.partial(span_rows, 1))
        stage(offsets - 1, 0, functools.partial(span_rows, 2))

        def body(pair, carry):
            order = 2 * pair
            stage(column(order), 1, functools.partial(moved_rows, ping), order + 1, pong)
            stage(column(order + 1), 0, functools.partial(moved_rows, pong), order + 2, ping)
            return carry

        lax.fori_loop(0, moved // 2 - 1, body, 0)
        stage(column(jnp.int32(moved - 2)), 1, functools.partial(moved_rows, ping), moved - 1, pong)
        stage(column(jnp.int32(moved - 1)), 0, functools.partial(moved_rows, pong))
        for place, row in enumerate(range(0, block, CHUNK)):
            if place < units:
                pltpu.matmul_push_rhs(linear_ref[...], 1, place)
            conv = pltpu.matmul_pop(sums[place]).astype(jnp.bfloat16)
            pltpu.matmul_acc_lhs(sums[place], conv, load_staged_rhs=1 if place < units else None)
        for place, row in enumerate(range(0, block, CHUNK)):
            summed[row : row + CHUNK, :] = pltpu.matmul_pop(sums[place])

    chunks = range(block // CHUNK)
    pl.run_scoped(accumulate, *[pltpu.ACC(place % units)((CHUNK, width), jnp.float32) for place in chunks])
    normed = layer_norm(summed[...])
    for piece in range(2):
        begin = 2 * (rows + begins[piece])
        own = [table[pl.ds(begin + side, segment, stride=2), :] for side in range(sides)]
        result = jnp.concatenate(own, axis=1) + normed[piece * segment : (piece + 1) * segment]
        out_ref[pl.ds(ends[piece], segment), :] = result.astype(jnp.bfloat16)


def position_conv(near, starts, stores, count, sources, parts, kept, olds, weight, linear):
    rows, offsets = near.shape
    channels = linear.shape[0]
    segment = rows // 8
    middle = offsets // 2
    steps = len(starts)
    row_id = jnp.arange(rows, dtype=jnp.int32)[:, None]
    index = 2 * jnp.where(near < 0, 3 * rows, near + row_id)
    index = jnp.concatenate([index[:, 1:middle], index[:, middle + 1 : offsets - 1]], axis=1)
    index = jnp.concatenate([index[begin : begin + segment] for pair in starts for begin in pair], axis=0)
    index = index.reshape(steps, 2 * segment, offsets - 3).transpose(0, 2, 1).reshape(steps, 1, -1)
    vmem = pl.BlockSpec(memory_space=pltpu.VMEM)
    return pl.pallas_call(
        functools.partial(conv_kernel, segment, starts, stores, sources, kept, rows),
        out_shape=jax.ShapeDtypeStruct((count, channels), jnp.bfloat16),
        grid=(steps,),
        in_specs=[pl.BlockSpec((1, 1, index.shape[2]), lambda step: (step, 0, 0), memory_space=pltpu.SMEM)]
        + [vmem] * (len(parts) + len(olds) + 2),
        out_specs=vmem,
        scratch_shapes=[
            pltpu.VMEM((6 * rows + 8, LANES), jnp.float32),
            pltpu.VMEM((4 * segment, LANES), jnp.float32),
            pltpu.VMEM((4 * segment, LANES), jnp.float32),
            pltpu.VMEM((2 * segment, channels), jnp.float32),
        ],
        compiler_params=pltpu.CompilerParams(vmem_limit_bytes=20 << 20),
        name="position_conv",
    )(index, *parts, *olds, weight, linear)


def on_device(
    points,
    qkv_one,
    proj_one,
    up_one,
    down_one,
    hilbert_device,
    hilbert_position,
    neighbors,
    conv_two,
    linear_two,
):
    row_count, channels = points.shape
    half = PATCH // 2
    devices = lax.axis_size(AXES)
    capacity = 2 * row_count // devices
    ring_up = [(i, (i + 1) % devices) for i in range(devices)]
    ring_down = [((i + 1) % devices, i) for i in range(devices)]
    before = lax.ppermute(points[row_count - half :], AXES, ring_up)
    behind = lax.ppermute(points[:half], AXES, ring_down)
    inner = inner_block(points, qkv_one, proj_one, up_one, down_one)
    inner, hilbert_device = lax.optimization_barrier((inner, hilbert_device))
    index, place = find_slots(hilbert_device, hilbert_position, devices, capacity)
    got_place = lax.all_to_all(place, AXES, split_axis=0, concat_axis=0, tiled=True)
    send = outer_block(
        index, before, points, behind, inner, qkv_one, proj_one, up_one, down_one, devices * capacity
    )
    got = lax.all_to_all(
        send.reshape(devices, capacity, channels), AXES, split_axis=0, concat_axis=0, tiled=True
    )
    segment = row_count // 8
    low, high = 3 * segment, 5 * segment
    spans = ((0, row_count), (low, row_count - low), (0, high), (0, low), (high, row_count - high))
    serial, upper_near, lower_near, lower_far, upper_far = settle(
        got_place, got.reshape(devices * capacity, channels), row_count, spans
    )
    left_near = lax.ppermute(upper_near, AXES, ring_up[:-1])
    right_near = lax.ppermute(lower_near, AXES, ring_down[:-1])
    left_far = lax.ppermute(lower_far, AXES, ring_up[:-1])
    right_far = lax.ppermute(upper_far, AXES, ring_down[:-1])
    parts = [left_near, serial, right_near]
    sources = [(low, row_count - low), (row_count, row_count), (2 * row_count, high)]
    inner = [(low, low + segment)]
    outer = [(0, segment), (2 * segment, high), (6 * segment, 7 * segment)]
    center = position_conv(
        neighbors, inner, [(0, segment)], 2 * segment, sources, parts, [], [], conv_two, linear_two
    )
    parts += [left_far, right_far]
    sources += [(0, low), (2 * row_count + high, row_count - high)]
    return position_conv(
        neighbors, outer, outer, row_count, sources, parts, [low], [center], conv_two, linear_two
    )


def solution(mesh):
    split = P(AXES)
    rows = P(AXES, None)
    return jax.shard_map(
        on_device,
        mesh=mesh,
        in_specs=(rows, P(), P(), P(), P(), split, split, rows, P(), P()),
        out_specs=rows,
        check_vma=False,
    )
```

```python
import functools

import jax
import jax.numpy as jnp
from jax import lax
from jax.experimental import pallas as pl
from jax.experimental.pallas import tpu as pltpu
from jax.sharding import PartitionSpec as P

HEADS = 16
HEAD_DIM = 16
PATCH = 1024
LANES = 128
EPS = 1e-05
LOG2E = 1.4426950408889634
AXES = ("curve", "group")


def layer_norm(values):
    values = values.astype(jnp.float32)
    center = jnp.mean(values, axis=-1, keepdims=True)
    offset = values - center
    spread = jnp.mean(offset * offset, axis=-1, keepdims=True)
    return offset * lax.rsqrt(spread + EPS)


def dot(left, right):
    return jnp.dot(left, right, preferred_element_type=jnp.float32)


def gelu(values):
    return 0.5 * values * (1.0 + lax.erf(values * 0.7071067811865476))


def slots_kernel(devices, capacity, device_ref, position_ref, index_ref, place_ref):
    rows = device_ref.shape[1]
    chunk = min(256, rows)
    row_id = lax.broadcasted_iota(jnp.int32, (chunk, chunk), 0)
    col_id = lax.broadcasted_iota(jnp.int32, (chunk, chunk), 1)
    before = (row_id <= col_id).astype(jnp.float32).astype(jnp.bfloat16)
    device_id = lax.broadcasted_iota(jnp.int32, (devices, chunk), 0)
    slot_id = lax.broadcasted_iota(jnp.int32, (capacity, chunk), 0)
    carry = jnp.zeros((devices, 1), jnp.float32)
    place = jnp.zeros((2 * devices, capacity), jnp.float32)
    for part in range(rows // chunk):
        span = slice(part * chunk, (part + 1) * chunk)
        target = device_ref[:, span]
        mine = (device_id == target).astype(jnp.float32)
        running = dot(mine.astype(jnp.bfloat16), before) + carry
        carry = running[:, chunk - 1 : chunk]
        slot = (jnp.sum(mine * running, axis=0, keepdims=True) - 1.0).astype(jnp.int32)
        index_ref[:, span] = 2 * (target * capacity + slot)
        code = position_ref[:, span] + 1
        high = mine * (code // LANES).astype(jnp.float32)
        low = mine * (code % LANES).astype(jnp.float32)
        here = (slot_id == slot).astype(jnp.float32).astype(jnp.bfloat16)
        place += lax.dot_general(
            jnp.concatenate([high, low], axis=0).astype(jnp.bfloat16),
            here,
            (((1,), (1,)), ((), ())),
            preferred_element_type=jnp.float32,
        )
    place_ref[...] = 2 * (place[:devices] * float(LANES) + place[devices:]).astype(jnp.int32)


def find_slots(device, position, devices, capacity):
    rows = device.shape[0]
    return pl.pallas_call(
        functools.partial(slots_kernel, devices, capacity),
        out_shape=(
            jax.ShapeDtypeStruct((1, rows), jnp.int32),
            jax.ShapeDtypeStruct((devices, capacity), jnp.int32),
        ),
        name="find_slots",
    )(device.reshape(1, rows), position.reshape(1, rows))


def project(source, key, value, weight_ref, key_ref, value_ref, query_ref=None, query=0):
    count, channels = source.shape
    normed = layer_norm(source).astype(jnp.bfloat16)
    key_ref[:, key : key + count] = lax.dot_general(
        weight_ref[:, channels : 2 * channels],
        normed,
        (((0,), (1,)), ((), ())),
        preferred_element_type=jnp.float32,
    ).astype(jnp.bfloat16)
    value_ref[value : value + count, :] = dot(normed, weight_ref[:, 2 * channels :]).astype(jnp.bfloat16)
    if query_ref is not None:
        query_ref[query : query + count, :] = dot(normed, weight_ref[:, :channels]).astype(jnp.bfloat16)


def transform(residual, first, start, query, key, value, proj_ref, up_ref, down_ref):
    half, channels = residual.shape
    per_group = LANES // HEAD_DIM
    head_of = lax.broadcasted_iota(jnp.int32, (1, LANES), 1) // HEAD_DIM
    scale = HEAD_DIM ** (-0.5) * LOG2E
    pieces = []
    for group in range(channels // LANES):
        lanes = slice(group * LANES, (group + 1) * LANES)
        queries = query[pl.ds(first, half), lanes]
        keys = key[lanes, pl.ds(start, PATCH)]
        values = value[pl.ds(start, PATCH), lanes]
        total = None
        for head in range(per_group):
            mine = head_of == head
            scores = dot(jnp.where(mine, queries, jnp.zeros_like(queries)), keys)
            peak = jnp.max(scores, axis=1, keepdims=True)
            weights = jnp.exp2((scores - peak) * scale).astype(jnp.bfloat16)
            ones = jnp.broadcast_to(mine.astype(jnp.float32).astype(jnp.bfloat16), values.shape)
            both = jnp.concatenate([jnp.where(mine, values, jnp.zeros_like(values)), ones], axis=1)
            result = dot(weights, both)
            total = result if total is None else total + result
        pieces.append((total[:, :LANES] / total[:, LANES:]).astype(jnp.bfloat16))
    mixed = jnp.concatenate(pieces, axis=1)
    after = (residual.astype(jnp.float32) + dot(mixed, proj_ref[...])).astype(jnp.bfloat16)
    normed = layer_norm(after).astype(jnp.bfloat16)
    hidden = gelu(dot(normed, up_ref[...])).astype(jnp.bfloat16)
    return (after.astype(jnp.float32) + dot(hidden, down_ref[...])).astype(jnp.bfloat16)


def inner_kernel(own_ref, qkv_ref, proj_ref, up_ref, down_ref, out_ref, query, key, value):
    step = pl.program_id(0)
    half = PATCH // 2
    steps = out_ref.shape[0] // half

    @pl.when(step == 0)
    def _():
        for part in range(steps):
            at = part * half
            project(own_ref[at + half : at + 2 * half, :], at, at, qkv_ref, key, value, query, at)

    first = pl.multiple_of(step * half, half)
    start = pl.multiple_of(PATCH * (step // 2), PATCH)
    residual = own_ref[pl.ds(first + half, half), :]
    out_ref[pl.ds(first, half), :] = transform(residual, first, start, query, key, value, proj_ref, up_ref, down_ref)


def outer_kernel(
    index_ref,
    left_ref,
    own_ref,
    right_ref,
    inner_ref,
    qkv_ref,
    proj_ref,
    up_ref,
    down_ref,
    send_ref,
    query,
    key,
    value,
    pairs,
    table,
):
    step = pl.program_id(0)
    rows = own_ref.shape[0]
    half = PATCH // 2

    def deliver(values, row):
        for side in range(2):
            pairs[pl.ds(side, half, stride=2), :] = values[:, side * LANES : (side + 1) * LANES].astype(jnp.float32)

        def body(part, carry):
            base = pl.multiple_of(part * LANES, LANES)
            for other in range(LANES):
                slot = pl.multiple_of(index_ref[0, row + base + other], 2)
                table[pl.ds(slot, 2), :] = pairs[pl.ds(2 * base + 2 * other, 2), :]
            return carry

        lax.fori_loop(0, half // LANES, body, 0)

    @pl.when(step == 0)
    def _():
        project(left_ref[...], 0, 0, qkv_ref, key, value)
        project(own_ref[:half, :], half, half, qkv_ref, key, value, query, 0)
        project(own_ref[rows - half :, :], 2 * half, 2 * half, qkv_ref, key, value, query, half)
        project(right_ref[...], 3 * half, 3 * half, qkv_ref, key, value)

        def body(part, carry):
            at = pl.multiple_of(part * half, half)
            deliver(inner_ref[pl.ds(at, half), :], at + half)
            return carry

        lax.fori_loop(0, inner_ref.shape[0] // half, body, 0)

    row = pl.multiple_of(step * (rows - half), half)
    first = pl.multiple_of(step * half, half)
    start = pl.multiple_of(step * PATCH, PATCH)
    residual = own_ref[pl.ds(row, half), :]
    deliver(transform(residual, first, start, query, key, value, proj_ref, up_ref, down_ref), row)

    @pl.when(step == pl.num_programs(0) - 1)
    def _():
        slots = send_ref.shape[0]
        for side in range(2):
            send_ref[:, side * LANES : (side + 1) * LANES] = table[pl.ds(side, slots, stride=2), :].astype(jnp.bfloat16)


def inner_block(own, qkv, proj, up, down):
    rows, channels = own.shape
    half = PATCH // 2
    count = rows - 2 * half
    vmem = pl.BlockSpec(memory_space=pltpu.VMEM)
    return pl.pallas_call(
        inner_kernel,
        out_shape=jax.ShapeDtypeStruct((count, channels), jnp.bfloat16),
        grid=(count // half,),
        in_specs=[vmem] * 5,
        out_specs=vmem,
        scratch_shapes=[
            pltpu.VMEM((count, channels), jnp.bfloat16),
            pltpu.VMEM((channels, count), jnp.bfloat16),
            pltpu.VMEM((count, channels), jnp.bfloat16),
        ],
        compiler_params=pltpu.CompilerParams(vmem_limit_bytes=56 << 20),
        name="inner_block",
    )(own, qkv, proj, up, down)


def outer_block(index, left, own, right, inner, qkv, proj, up, down, slots):
    channels = own.shape[1]
    half = PATCH // 2
    vmem = pl.BlockSpec(memory_space=pltpu.VMEM)
    return pl.pallas_call(
        outer_kernel,
        out_shape=jax.ShapeDtypeStruct((slots, channels), jnp.bfloat16),
        grid=(2,),
        in_specs=[pl.BlockSpec(memory_space=pltpu.SMEM)] + [vmem] * 8,
        out_specs=vmem,
        scratch_shapes=[
            pltpu.VMEM((2 * half, channels), jnp.bfloat16),
            pltpu.VMEM((channels, 2 * PATCH), jnp.bfloat16),
            pltpu.VMEM((2 * PATCH, channels), jnp.bfloat16),
            pltpu.VMEM((2 * half, LANES), jnp.float32),
            pltpu.VMEM((2 * slots, LANES), jnp.float32),
        ],
        compiler_params=pltpu.CompilerParams(vmem_limit_bytes=56 << 20),
        name="outer_block",
    )(index, left, own, right, inner, qkv, proj, up, down)


def settle_kernel(spans, place_ref, got_ref, *refs):
    outs, (pairs, table) = refs[: len(spans)], refs[len(spans) :]
    slots = got_ref.shape[0]
    capacity = place_ref.shape[1]
    for side in range(2):
        pairs[pl.ds(side, slots, stride=2), :] = got_ref[:, side * LANES : (side + 1) * LANES].astype(jnp.float32)

    def body(source, carry):
        base = pl.multiple_of(source * (2 * capacity), 2 * capacity)
        for slot in range(capacity):
            target = pl.multiple_of(place_ref[source, slot] + 6, 2)
            table[pl.ds(target, 2), :] = pairs[pl.ds(base + 2 * slot, 2), :]
        return carry

    lax.fori_loop(0, place_ref.shape[0], body, 0)
    for (first, count), out_ref in zip(spans, outs):
        for side in range(2):
            out_ref[:, side * LANES : (side + 1) * LANES] = table[
                pl.ds(8 + 2 * first + side, count, stride=2), :
            ].astype(jnp.bfloat16)


def settle(place, got, rows, spans):
    slots, channels = got.shape
    vmem = pl.BlockSpec(memory_space=pltpu.VMEM)
    return pl.pallas_call(
        functools.partial(settle_kernel, spans),
        out_shape=tuple(jax.ShapeDtypeStruct((count, channels), jnp.bfloat16) for _, count in spans),
        in_specs=[pl.BlockSpec(memory_space=pltpu.SMEM), vmem],
        out_specs=(vmem,) * len(spans),
        scratch_shapes=[pltpu.VMEM((2 * slots, LANES), jnp.float32), pltpu.VMEM((2 * rows + 8, LANES), jnp.float32)],
        compiler_params=pltpu.CompilerParams(vmem_limit_bytes=56 << 20),
        name="settle",
    )(place, got)


CHUNK = 32


def pick(step, values):
    return sum(jnp.where(step == place, value, 0) for place, value in enumerate(values) if value)


def conv_kernel(segment, starts, stores, sources, kept, rows, index_ref, *refs):
    parts, refs = refs[: len(sources)], refs[len(sources) :]
    olds, refs = refs[: len(kept)], refs[len(kept) :]
    weight_ref, linear_ref, out_ref, table, ping, pong, summed, arrived, *stages = refs
    step = pl.program_id(0)
    width = out_ref.shape[1]
    offsets = weight_ref.shape[0] // width
    middle = offsets // 2
    moved = offsets - 3
    block = 2 * segment
    sides = width // LANES
    units = 2

    @pl.when(step == 0)
    def _():
        copies = [
            pltpu.make_async_copy(ref, stage, arrived.at[place])
            for place, (ref, stage) in enumerate(zip(parts, stages))
        ]
        for copy in copies:
            copy.start()
        for (first, count), ref, copy in zip(sources, stages, copies):
            copy.wait()
            for side in range(sides):
                table[pl.ds(2 * first + side, count, stride=2), :] = ref[:, side * LANES : (side + 1) * LANES].astype(
                    jnp.float32
                )
        table[pl.ds(6 * rows, 8), :] = jnp.zeros((8, LANES), jnp.float32)
        for first, ref in zip(kept, olds):
            out_ref[first : first + ref.shape[0], :] = ref[...]

    begins = [pl.multiple_of(pick(step, [pair[piece] for pair in starts]), segment) for piece in range(2)]
    ends = [pl.multiple_of(pick(step, [pair[piece] for pair in stores]), segment) for piece in range(2)]

    def fetch(order, buffer, row):
        for other in range(row, row + CHUNK):
            source = pl.multiple_of(index_ref[0, 0, order * block + other], 2)
            buffer[2 * other : 2 * other + 2, :] = table[pl.ds(source, 2), :]

    def moved_rows(buffer, row):
        return [buffer[pl.ds(2 * row + side, CHUNK, stride=2), :] for side in range(sides)]

    def span_rows(span, row):
        begin = 2 * (span * rows + begins[row // segment] + row % segment)
        return [table[pl.ds(begin + side, CHUNK, stride=2), :] for side in range(sides)]

    def column(order):
        return order + jnp.where(order < middle - 1, 1, 2)

    def accumulate(*sums):
        def stage(offset, staging, take, order=None, buffer=None):
            weight = weight_ref[pl.ds(pl.multiple_of(offset * width, width), width), :]
            for unit in range(units):
                pltpu.matmul_push_rhs(weight, staging, unit)
            for place, row in enumerate(range(0, block, CHUNK)):
                if buffer is not None:
                    fetch(order, buffer, row)
                left = jnp.concatenate([half.astype(jnp.bfloat16) for half in take(row)], axis=1)
                pltpu.matmul_acc_lhs(sums[place], left, load_staged_rhs=staging if place < units else None)

        for place, row in enumerate(range(0, block, CHUNK)):
            summed[row : row + CHUNK, :] = pltpu.matmul_pop(sums[place])
        stage(0, 0, functools.partial(span_rows, 0), 0, ping)
        stage(middle, 1, functools.partial(span_rows, 1))
        stage(offsets - 1, 0, functools.partial(span_rows, 2))

        def body(pair, carry):
            order = 2 * pair
            stage(column(order), 1, functools.partial(moved_rows, ping), order + 1, pong)
            stage(column(order + 1), 0, functools.partial(moved_rows, pong), order + 2, ping)
            return carry

        lax.fori_loop(0, moved // 2 - 1, body, 0)
        stage(column(jnp.int32(moved - 2)), 1, functools.partial(moved_rows, ping), moved - 1, pong)
        stage(column(jnp.int32(moved - 1)), 0, functools.partial(moved_rows, pong))
        for place, row in enumerate(range(0, block, CHUNK)):
            if place < units:
                pltpu.matmul_push_rhs(linear_ref[...], 1, place)
            conv = pltpu.matmul_pop(sums[place]).astype(jnp.bfloat16)
            pltpu.matmul_acc_lhs(sums[place], conv, load_staged_rhs=1 if place < units else None)
        for place, row in enumerate(range(0, block, CHUNK)):
            summed[row : row + CHUNK, :] = pltpu.matmul_pop(sums[place])

    chunks = range(block // CHUNK)
    pl.run_scoped(accumulate, *[pltpu.ACC(place % units)((CHUNK, width), jnp.float32) for place in chunks])
    normed = layer_norm(summed[...])
    for piece in range(2):
        begin = 2 * (rows + begins[piece])
        own = [table[pl.ds(begin + side, segment, stride=2), :] for side in range(sides)]
        result = jnp.concatenate(own, axis=1) + normed[piece * segment : (piece + 1) * segment]
        out_ref[pl.ds(ends[piece], segment), :] = result.astype(jnp.bfloat16)


def position_conv(near, starts, stores, count, sources, parts, kept, olds, weight, linear):
    rows, offsets = near.shape
    channels = linear.shape[0]
    segment = rows // 8
    middle = offsets // 2
    steps = len(starts)
    row_id = jnp.arange(rows, dtype=jnp.int32)[:, None]
    index = 2 * jnp.where(near < 0, 3 * rows, near + row_id)
    index = jnp.concatenate([index[:, 1:middle], index[:, middle + 1 : offsets - 1]], axis=1)
    index = jnp.concatenate([index[begin : begin + segment] for pair in starts for begin in pair], axis=0)
    index = index.reshape(steps, 2 * segment, offsets - 3).transpose(0, 2, 1).reshape(steps, 1, -1)
    vmem = pl.BlockSpec(memory_space=pltpu.VMEM)
    return pl.pallas_call(
        functools.partial(conv_kernel, segment, starts, stores, sources, kept, rows),
        out_shape=jax.ShapeDtypeStruct((count, channels), jnp.bfloat16),
        grid=(steps,),
        in_specs=[pl.BlockSpec((1, 1, index.shape[2]), lambda step: (step, 0, 0), memory_space=pltpu.SMEM)]
        + [pl.BlockSpec(memory_space=pl.ANY)] * len(parts)
        + [vmem] * (len(olds) + 2),
        out_specs=vmem,
        scratch_shapes=[
            pltpu.VMEM((6 * rows + 8, LANES), jnp.float32),
            pltpu.VMEM((4 * segment, LANES), jnp.float32),
            pltpu.VMEM((4 * segment, LANES), jnp.float32),
            pltpu.VMEM((2 * segment, channels), jnp.float32),
            pltpu.SemaphoreType.DMA((len(parts),)),
        ]
        + [pltpu.VMEM(part.shape, part.dtype) for part in parts],
        compiler_params=pltpu.CompilerParams(vmem_limit_bytes=20 << 20),
        name="position_conv",
    )(index, *parts, *olds, weight, linear)


def on_device(
    points,
    qkv_one,
    proj_one,
    up_one,
    down_one,
    hilbert_device,
    hilbert_position,
    neighbors,
    conv_two,
    linear_two,
):
    row_count, channels = points.shape
    half = PATCH // 2
    devices = lax.axis_size(AXES)
    capacity = 2 * row_count // devices
    ring_up = [(i, (i + 1) % devices) for i in range(devices)]
    ring_down = [((i + 1) % devices, i) for i in range(devices)]
    before = lax.ppermute(points[row_count - half :], AXES, ring_up)
    behind = lax.ppermute(points[:half], AXES, ring_down)
    inner = inner_block(points, qkv_one, proj_one, up_one, down_one)
    inner, hilbert_device = lax.optimization_barrier((inner, hilbert_device))
    index, place = find_slots(hilbert_device, hilbert_position, devices, capacity)
    got_place = lax.all_to_all(place, AXES, split_axis=0, concat_axis=0, tiled=True)
    send = outer_block(
        index, before, points, behind, inner, qkv_one, proj_one, up_one, down_one, devices * capacity
    )
    got = lax.all_to_all(
        send.reshape(devices, capacity, channels), AXES, split_axis=0, concat_axis=0, tiled=True
    )
    segment = row_count // 8
    low, high = 3 * segment, 5 * segment
    spans = ((0, row_count), (low, row_count - low), (0, high), (0, low), (high, row_count - high))
    serial, upper_near, lower_near, lower_far, upper_far = settle(
        got_place, got.reshape(devices * capacity, channels), row_count, spans
    )
    left_near = lax.ppermute(upper_near, AXES, ring_up[:-1])
    right_near = lax.ppermute(lower_near, AXES, ring_down[:-1])
    left_far = lax.ppermute(lower_far, AXES, ring_up[:-1])
    right_far = lax.ppermute(upper_far, AXES, ring_down[:-1])
    parts = [left_near, serial, right_near]
    sources = [(low, row_count - low), (row_count, row_count), (2 * row_count, high)]
    inner = [(low, low + segment)]
    outer = [(0, segment), (2 * segment, high), (6 * segment, 7 * segment)]
    center = position_conv(
        neighbors, inner, [(0, segment)], 2 * segment, sources, parts, [], [], conv_two, linear_two
    )
    parts += [left_far, right_far]
    sources += [(0, low), (2 * row_count + high, row_count - high)]
    return position_conv(
        neighbors, outer, outer, row_count, sources, parts, [low], [center], conv_two, linear_two
    )


def solution(mesh):
    split = P(AXES)
    rows = P(AXES, None)
    return jax.shard_map(
        on_device,
        mesh=mesh,
        in_specs=(rows, P(), P(), P(), P(), split, split, rows, P(), P()),
        out_specs=rows,
        check_vma=False,
    )
```
